32 devices in a mesh: groups: 2 (over x), pairs: 8 (over z, y), mp: 2 (over core).
Axes of the slice: x: 2, y: 2, z: 4, core: 2. Of those that a mesh axis runs over, the one named last changes fastest.
Arguments:
- tokens: bfloat16 [64, 196, 768], P(('groups', 'pairs'), None, 'mp'), parts along dimension 0, may hold values from -6 to 6
- gain_query: float32 [768], replicated, may hold values from 0.25 to 1.75
- gain_context: float32 [768], replicated, may hold values from 0.25 to 1.75
- query_weight: bfloat16 [768, 768], replicated, may hold values from -1 to 1
- key_weight: bfloat16 [768, 768], replicated, may hold values from -8 to 8
- value_weight: bfloat16 [768, 768], replicated, may hold values from -0.21875 to 0.21875
- out_weight: bfloat16 [768, 768], replicated, may hold values from -0.21875 to 0.21875
- gain_head: float32 [768], replicated, may hold values from 0.25 to 1.75
- hidden_weight: bfloat16 [768, 1024], replicated, may hold values from -0.21875 to 0.21875
- hidden_bias: float32 [1024], replicated, may hold values from -3 to 3
- point_weight: bfloat16 [4, 1024], replicated, may hold values from -0.1875 to 0.1875
- view_owner: int32 [192, 1], P('groups'), parts along dimension 0, may hold values from 0 to 7; in each aligned block of 12 rows (0 to 11, 12 to 23, ...) at most 2 rows name the same one
- view_local: int32 [192], P('groups'), parts along dimension 0, may hold values from 0 to 3
- pair_count: int32 [16], P('groups'), parts along dimension 0, may hold values from 1 to 6, 24 in all
Outputs:
- joined: float32 [64, 4, 196], P(('groups', 'pairs', 'mp')), parts along dimension 0
The draws below stay inside these ranges and needn't reach their ends.
There are 2 independent parts, one for each index of `groups`. The reference program is written for one: setup_inputs(seed, part) draws one part's arguments, and reference() takes and returns one part's arrays. A program takes and returns all parts, laid end to end along the dimension named above; an argument that names none is the same for every part. Nothing has to cross between parts.
Inputs may be any that keep to these rules, and one draw needn't show every extreme that they name: `view_owner`: among the 12 views of one worker no owner appears more than 2 times, and in every draw some owner appears exactly 2 times. `pair_count`: some worker has exactly 6 pairs in every draw; the counts sum to 24.
All inputs are finite; a program needn't handle non-finite values.
Results may differ from the reference program's by a relative error of at most 0.012.
The reference program's roundings to bfloat16 on the way count: a program that leaves them out, or rounds other values in their place, can miss the bound.
Values may be sent and summed in bfloat16 or wider, within the bound.
No kernel may reach another device: no remote copies, remote signals or barrier semaphores. Data moves between devices by JAX's collectives and lax.ppermute only.
A program may use at most 128 MiB of HBM per device.

```python
import math
import jax
import jax.numpy as jnp
import numpy as np
from jax import lax

D = 768
HEADS = 12
TOK = 196
HID = 1024
IMG_DEV = 4
PAIR_DEV = 3
CAP = 6
REACH = 2
IMAGES = 32
SLOTS = 48
N_PAIRS = 8


def shared_weight(key):
    return jax.random.normal(jax.random.fold_in(key, 11), (D, D), jnp.float32) / math.sqrt(D)


def draw_query_weight(key, part):
    return jnp.clip(shared_weight(key), -1.0, 1.0).astype(jnp.bfloat16)


def draw_key_weight(key, part):
    fresh = jax.random.normal(jax.random.fold_in(key, 12), (D, D), jnp.float32) / math.sqrt(D)
    return jnp.clip(fresh, -1.0, 1.0).astype(jnp.bfloat16)


def draw_tokens(key, part):
    base_draw = jax.random.normal(jax.random.fold_in(key, 1), (IMAGES, TOK, D), jnp.float32)
    return jnp.clip(base_draw, -6.0, 6.0).astype(jnp.bfloat16)


def plant(array, own_key, smallest, high):
    longest = array.shape.index(max(array.shape))
    spots = []
    for shift in (0, 1):
        where = [jax.random.randint(jax.random.fold_in(own_key, axis), (), 0, length) for axis, length in enumerate(array.shape)]
        where[longest] = (where[longest] + shift) % array.shape[longest]
        spots.append(tuple(where))
    return array.at[spots[0]].set(smallest).at[spots[1]].set(high)


def split_up(number_of, total, reach, lean):
    portions = [(1 << 20) // math.isqrt(standing ** lean) + 1 for standing in range(2, number_of + 1)]
    rest, holding = total - reach - (number_of - 1), [1] * (number_of - 1)
    while rest > 0:
        candidates = [i for i in range(number_of - 1) if holding[i] < reach]
        pool, budget = sum([portions[i] for i in candidates]), rest
        for i in candidates:
            more = min(reach - holding[i], max(1, budget * portions[i] // pool), rest)
            holding[i] = holding[i] + more
            rest = rest - more
    return np.array([reach] + holding)


def ragged(key, count, total, limit, slope):
    if count == 2:
        one = jax.random.randint(key, (), max(1, total - limit), min(limit, total - 1) + 1)
        return jnp.stack([one, total - one])
    lengths = jnp.asarray(split_up(count, total, limit, slope), jnp.int32)
    couples = (count - 1) // 2
    giver, receiver = lengths[1:1 + 2 * couples:2], lengths[2:2 + 2 * couples:2]
    room = jnp.minimum(giver - 1, limit - receiver)
    shifted = jax.random.randint(jax.random.fold_in(key, 1), (couples,), 0, 1 << 20) % (room + 1)
    lengths = lengths.at[1:1 + 2 * couples:2].set(giver - shifted).at[2:2 + 2 * couples:2].set(receiver + shifted)
    return lengths[jax.random.permutation(jax.random.fold_in(key, 2), count)]


def deal_out(rng, own, number, rows, amount, top, reach, lean):
    ranking = jax.random.permutation(rng, amount)
    crowded, common = portions_of(amount, rows * top, reach, lean, True), portions_of(amount, rows * top, reach, lean, False)
    places = jnp.arange(amount)

    def named(sizes, turn):
        used = int((sizes > 0).sum())
        fixed = max(1, used // 4)
        moved = fixed + (places - fixed + turn * (used - fixed)) % max(1, amount - fixed)
        return jnp.zeros((amount,), jnp.int32).at[ranking[jnp.where(places < fixed, places, moved)]].set(jnp.asarray(sizes, jnp.int32))

    sizes = jnp.where(number % 4 == 0, named(crowded, number // 4), named(common, number - number // 4 - 1))
    mixed = jax.random.permutation(jax.random.fold_in(own, 3), amount)
    source_of, taker = mixed[0:amount // 2 * 2:2], mixed[1:amount // 2 * 2:2]
    room = jnp.minimum(sizes[source_of] - 1, reach - sizes[taker]) // 2
    room = jnp.where((source_of == ranking[0]) | (taker == ranking[0]) | (sizes[taker] == 0), 0, jnp.maximum(room, 0))
    moved = jax.random.randint(jax.random.fold_in(own, 4), (amount // 2,), 0, 1 << 20) % (room + 1)
    sizes = sizes.at[source_of].add(-moved).at[taker].add(moved)
    members = jnp.searchsorted(jnp.cumsum(sizes), jnp.arange(rows * top), side="right").astype(jnp.int32)
    listing = members.reshape(top, rows).T
    listing = listing[jax.random.permutation(jax.random.fold_in(own, 1), rows)]
    turn = jax.random.randint(jax.random.fold_in(own, 2), (rows, 1), 0, top)
    return jnp.take_along_axis(listing, (jnp.arange(top)[None, :] + turn) % top, axis=1)


def portions_of(count, total, reach, lean, full):
    loads = [(1 << 20) // math.isqrt(grade ** lean) + 1 for grade in range(1, count + 1)]
    largest = reach if full else min(reach, max(-(-total // count), total * loads[0] // sum(loads)))
    least = 1 if total - largest >= count - 1 else 0
    holding, spare = [largest] + [least] * (count - 1), total - largest - least * (count - 1)
    while spare > 0:
        free = [i for i in range(1, count) if holding[i] < largest] or [i for i in range(1, count) if holding[i] < reach]
        whole, left = sum([loads[i] for i in free]), spare
        for i in free:
            extra = min(reach - holding[i], max(1, left * loads[i] // whole), spare)
            holding[i] = holding[i] + extra
            spare = spare - extra
    return np.array(holding)


def normal_values(stream_key, shape, spread, most, dtype=jnp.bfloat16):
    values = jax.random.normal(stream_key, shape, jnp.float32) * spread
    return jnp.minimum(jnp.maximum(values, -most), most).astype(dtype)


def setup_inputs(seed: int = 0, part: int = 0) -> dict:
    key_of = jax.random.split(jax.random.key(seed), 15)
    own_keys = jax.random.split(jax.random.fold_in(key_of[14], part), 15)
    tokens = draw_tokens(jax.random.fold_in(jax.random.fold_in(key_of[14], part), 71), part)
    gain_query = jnp.clip(1.0 + 0.15 * jax.random.normal(key_of[1], (D,), jnp.float32), 0.25, 1.75)
    gain_context = jnp.clip(1.0 + 0.15 * jax.random.normal(key_of[2], (D,), jnp.float32), 0.25, 1.75)
    query_weight = draw_query_weight(jax.random.fold_in(key_of[14], 71), part)
    key_weight = draw_key_weight(jax.random.fold_in(key_of[14], 71), part)
    value_weight = normal_values(key_of[5], (D, D), D ** -0.5, 0.21875)
    out_weight = normal_values(key_of[6], (D, D), D ** -0.5, 0.21875)
    gain_head = jnp.clip(1.0 + 0.15 * jax.random.normal(key_of[7], (D,), jnp.float32), 0.25, 1.75)
    hidden_weight = normal_values(key_of[8], (D, HID), D ** -0.5, 0.21875)
    hidden_bias = normal_values(key_of[9], (HID,), 0.5, 3.0, jnp.float32)
    point_weight = normal_values(key_of[10], (4, HID), HID ** -0.5, 0.1875)
    view_owner_keys = jax.random.split(jax.random.fold_in(own_keys[11], 1), (2 * SLOTS) // (2 * CAP))
    view_owner_turns = jax.random.permutation(jax.random.fold_in(own_keys[11], 3), (2 * SLOTS) // (2 * CAP))
    view_owner = jax.vmap(lambda own, number: deal_out(jax.random.fold_in(own_keys[11], 2), own, number, 2 * CAP, N_PAIRS, 1, REACH, 2))(view_owner_keys, view_owner_turns).reshape((2 * SLOTS, 1))
    view_local = plant(jax.random.randint(own_keys[12], (2 * SLOTS,), 0, IMG_DEV), jax.random.fold_in(own_keys[12], 1), 0, IMG_DEV - 1).astype(jnp.int32)
    pair_count = ragged(own_keys[13], N_PAIRS, PAIR_DEV * N_PAIRS, CAP, 2).astype(jnp.int32)
    return dict(tokens=tokens, gain_query=gain_query, gain_context=gain_context, query_weight=query_weight, key_weight=key_weight, value_weight=value_weight, out_weight=out_weight, gain_head=gain_head, hidden_weight=hidden_weight, hidden_bias=hidden_bias, point_weight=point_weight, view_owner=view_owner, view_local=view_local, pair_count=pair_count)


EPS = 1e-06

def norm_rows(rows_in, gain_vec):
    rows_in = rows_in.astype(jnp.float32)
    average = lax.optimization_barrier(jnp.mean(rows_in, axis=-1, keepdims=True))
    centered = rows_in - average
    variance = lax.optimization_barrier(jnp.mean(centered * centered, axis=-1, keepdims=True))
    return (centered * lax.rsqrt(variance + EPS) * gain_vec).astype(jnp.bfloat16)

def project(rows_in, weight):
    return jnp.einsum('vtd,de->vte', rows_in.astype(jnp.float32), weight.astype(jnp.float32))

def attention(queries, key_rows, value_rows):
    view_count, token_count, feature_width = queries.shape
    head_size = feature_width // HEADS
    split_shape = (view_count, token_count, HEADS, head_size)
    scores = jnp.einsum('vqhd,vkhd->vhqk', queries.reshape(split_shape).astype(jnp.float32), key_rows.reshape(split_shape).astype(jnp.float32)) / math.sqrt(head_size)
    row_max = lax.optimization_barrier(jnp.max(scores, axis=-1, keepdims=True))
    exponent = jnp.exp(scores - row_max)
    attn_probs = (exponent / lax.optimization_barrier(jnp.sum(exponent, axis=-1, keepdims=True))).astype(jnp.bfloat16)
    blended = jnp.einsum('vhqk,vkhd->vqhd', attn_probs.astype(jnp.float32), value_rows.reshape(split_shape).astype(jnp.float32))
    return blended.astype(jnp.bfloat16).reshape(view_count, token_count, feature_width)

def decode(query_views, context_views, gain_query, gain_context, query_weight, key_weight, value_weight, out_weight, gain_head, hidden_weight, hidden_bias, point_weight):
    query_in = norm_rows(query_views, gain_query)
    context_in = norm_rows(context_views, gain_context)
    query_proj = project(query_in, query_weight).astype(jnp.bfloat16)
    key_proj = project(context_in, key_weight).astype(jnp.bfloat16)
    value_proj = project(context_in, value_weight).astype(jnp.bfloat16)
    attended = attention(query_proj, key_proj, value_proj)
    updated = query_views.astype(jnp.float32) + project(attended, out_weight)
    head_in = norm_rows(updated, gain_head)
    hidden = jax.nn.gelu(project(head_in, hidden_weight) + hidden_bias).astype(jnp.bfloat16)
    head_out = jnp.einsum('vth,ch->vct', hidden.astype(jnp.float32), point_weight.astype(jnp.float32))
    confidence = 1.0 + jnp.exp(head_out[:, 3:4])
    return jnp.concatenate([head_out[:, :3] * confidence, confidence], axis=1)

def reference(tokens, gain_query, gain_context, query_weight, key_weight, value_weight, out_weight, gain_head, hidden_weight, hidden_bias, point_weight, view_owner, view_local, pair_count):
    request_count = 2 * CAP
    image_rows = (view_owner[:, 0] * IMG_DEV + view_local).astype(jnp.int32).reshape(N_PAIRS, request_count)

    def worker(worker_item):
        row_ids, pair_total = worker_item
        view_rows = tokens[row_ids]
        partner = view_rows.reshape(CAP, 2, TOK, D)[:, ::-1].reshape(request_count, TOK, D)
        contrib = decode(view_rows, partner, gain_query, gain_context, query_weight, key_weight, value_weight, out_weight, gain_head, hidden_weight, hidden_bias, point_weight)
        live_mask = (jnp.arange(request_count) // 2 < pair_total).astype(jnp.float32)
        return contrib * live_mask[:, None, None]
    contribs = lax.map(worker, (image_rows, pair_count))
    return jax.ops.segment_sum(contribs.reshape(N_PAIRS * request_count, 4, TOK), image_rows.reshape(-1), num_segments=IMAGES)
```

```python
import functools

import jax
import jax.numpy as jnp
from jax import lax
from jax.experimental import pallas as pl
from jax.experimental.pallas import tpu as pltpu
from jax.sharding import PartitionSpec as P

HEADS = 12
EPS = 1e-06
F32 = jnp.float32
BF16 = jnp.bfloat16


def ring_place(index, count):
    if count > 8:
        return index
    half = index // 2
    return jnp.where(index % 2 == 0, half, count - 1 - half)


def ring_order(count):
    if count > 8:
        return list(range(count))
    return list(range(0, count, 2)) + list(range(count - 1, 0, -2))


def ring_gather(shard, count):
    order = ring_order(count)
    ahead = [(order[i], order[(i + 1) % count]) for i in range(count)]
    back = [(b, a) for a, b in ahead]
    middle = count // 2
    half = shard.shape[0] // 2
    parts = [None] * (count + 1)
    parts[0] = shard
    going, coming = shard, shard
    for step in range(1, middle):
        going = lax.ppermute(going, "pairs", ahead)
        coming = lax.ppermute(coming, "pairs", back)
        parts[count - step] = going
        parts[step] = coming
    parts[middle] = lax.ppermute(going[:half], "pairs", ahead)
    parts[count] = lax.ppermute(coming[half:], "pairs", back)
    return parts


def plan(owners, locals_, counts, worker, core, image_count, worker_count):
    requests = locals_.shape[0] // worker_count
    share = requests // 4
    first = jnp.array([0, 1, 2, 3, 4, 5, 3, 2], jnp.int32)
    second = jnp.array([4, 5, 3, 2, 0, 1, 2, 3], jnp.int32)
    place = jnp.where(core == 0, first, second)
    pair = worker * share + place // 2
    workers = jnp.arange(worker_count, dtype=jnp.int32)
    upto = jnp.sum(
        jnp.where(workers[None, :] <= workers[:, None], counts[None, :], 0), axis=1
    )
    past = upto[None, :] <= pair[:, None]
    holder = jnp.sum(past.astype(jnp.int32), axis=1)
    slot = pair - jnp.sum(jnp.where(past, counts[None, :], 0), axis=1)
    view = holder * requests + slot * 2 + place % 2
    all_images = owners * image_count + locals_
    ids = jnp.arange(all_images.shape[0], dtype=jnp.int32)
    image = jnp.sum(jnp.where(view[:, None] == ids[None, :], all_images[None, :], 0), axis=1)
    owner, row = image // image_count, image % image_count
    gap = (ring_place(owner, worker_count) - ring_place(worker, worker_count)) % worker_count
    middle, half = worker_count // 2, image_count // 2
    late = jnp.logical_and(gap == middle, row >= half)
    part = jnp.where(late, worker_count, gap)
    row = jnp.where(late, row - half, row)
    head = jnp.broadcast_to(jnp.asarray(core, jnp.int32), (8,))
    return jnp.stack([part, row, image, head])


def fetch(table, column, parts, target, sem, wait):
    if wait:
        pltpu.make_async_copy(parts[0].at[0], target, sem).wait()
        return
    part, row = table[0, column], table[1, column]
    for k, source in enumerate(parts):

        @pl.when(part == k)
        def _():
            pltpu.make_async_copy(source.at[row], target, sem).start()


def pick_kernel(count, table, *refs):
    parts, out, sems = refs[:count], refs[count], refs[count + 1]
    for wait in (False, True):
        for j in range(4):
            fetch(table, 4 + j, parts, out.at[j], sems.at[j], wait)


def norm_last(rows, gain):
    average = jnp.mean(rows, axis=-1, keepdims=True)
    centered = rows - average
    variance = jnp.mean(centered * centered, axis=-1, keepdims=True)
    return centered * lax.rsqrt(variance + EPS) * gain


def decode_kernel(count, tokens, table, *refs):
    parts = refs[:count]
    (other, gain_q, gain_c, gain_h, bias_h, wp) = refs[count : count + 6]
    weights = refs[count + 6 : count + 11]
    out = refs[count + 11]
    (mine, theirs, xq, xc, res, q, k, v, att, hid) = refs[count + 12 : count + 22]
    held = refs[count + 22 : count + 27]
    sems, wsems, osem = refs[count + 27 :]
    wq, wk, wv, wo, wh = held
    rows, half = mine.shape[1], mine.shape[2]
    views, padded, width = q.shape
    core = table[3, 0]

    for j in range(4):
        fetch(table, j, parts, mine.at[j], sems.at[j], False)
    incoming = pltpu.make_async_copy(other, theirs, osem)
    incoming.start()
    copies = [
        pltpu.make_async_copy(weights[i], held[i], wsems.at[i]) for i in range(len(weights))
    ]
    for copy in copies:
        copy.start()

    out[...] = jnp.zeros_like(out)
    tail = jnp.zeros((views, padded - rows, width), BF16)
    xq[:, rows:, :] = tail
    xc[:, rows:, :] = tail
    res[:, rows:, :] = tail
    for j in range(4):
        fetch(table, j, parts, mine.at[j], sems.at[j], True)
    incoming.wait()

    here = pl.ds(pl.multiple_of(core * half, half), half)
    there = pl.ds(pl.multiple_of((1 - core) * half, half), half)
    context_of = (1, 0, None, 2)
    for j in range(4):
        raw_a, raw_b = mine[j], theirs[j]
        a, b = raw_a.astype(F32), raw_b.astype(F32)
        average = (
            jnp.sum(a, axis=-1, keepdims=True) + jnp.sum(b, axis=-1, keepdims=True)
        ) / width
        a, b = a - average, b - average
        variance = (
            jnp.sum(a * a, axis=-1, keepdims=True) + jnp.sum(b * b, axis=-1, keepdims=True)
        ) / width
        scale = lax.rsqrt(variance + EPS)
        a, b = a * scale, b * scale
        if j < views:
            xq[j, :rows, here] = (a * gain_q[:, here]).astype(BF16)
            xq[j, :rows, there] = (b * gain_q[:, there]).astype(BF16)
            res[j, :rows, here] = raw_a
            res[j, :rows, there] = raw_b
        if context_of[j] is not None:
            xc[context_of[j], :rows, here] = (a * gain_c[:, here]).astype(BF16)
            xc[context_of[j], :rows, there] = (b * gain_c[:, there]).astype(BF16)

    total = views * padded
    head_size = width // HEADS
    queries = xq[...].reshape(total, width)
    contexts = xc[...].reshape(total, width)
    copies[0].wait()
    proj = jnp.dot(queries, wq[...], preferred_element_type=F32)
    q[...] = (proj.astype(BF16) * BF16(head_size**-0.5)).reshape(views, padded, width)
    copies[1].wait()
    proj = jnp.dot(contexts, wk[...], preferred_element_type=F32)
    k[...] = proj.astype(BF16).reshape(views, padded, width)
    copies[2].wait()
    proj = jnp.dot(contexts, wv[...], preferred_element_type=F32)
    v[...] = proj.astype(BF16).reshape(views, padded, width)

    block = 2 * head_size
    low = lax.broadcasted_iota(jnp.int32, (padded, block), 1) < head_size
    hide = jnp.where(lax.broadcasted_iota(jnp.int32, (1, padded), 1) < tokens, 0.0, -1e30)
    nothing = jnp.zeros((padded, block), BF16)

    def attend(i, carry):
        for b in range(width // block):
            cols = slice(b * block, (b + 1) * block)
            qb, kb, vb = q[i, :, cols], k[i, :, cols], v[i, :, cols]
            blended = []
            for keep in (0, 1):
                qh = jnp.where(low, qb, nothing) if keep == 0 else jnp.where(low, nothing, qb)
                scores = lax.dot_general(
                    qh, kb, (((1,), (1,)), ((), ())), preferred_element_type=F32
                )
                scores = scores + hide
                peak = jnp.max(scores, axis=-1, keepdims=True)
                expo = jnp.exp(scores - peak)
                inverse = 1.0 / jnp.sum(expo, axis=-1, keepdims=True)
                probs = (expo * inverse).astype(BF16)
                blended.append(jnp.dot(probs, vb, preferred_element_type=F32))
            att[i, :, cols] = jnp.where(low, blended[0], blended[1]).astype(BF16)
        return carry

    lax.fori_loop(0, views, attend, 0)

    copies[3].wait()
    updated = jnp.dot(att[...].reshape(total, width), wo[...], preferred_element_type=F32)
    updated = updated + res[...].reshape(total, width).astype(F32)
    head_in = norm_last(updated, gain_h[...]).astype(BF16)
    copies[4].wait()
    hidden = jnp.dot(head_in, wh[...], preferred_element_type=F32) + bias_h[...]
    hid[...] = jax.nn.gelu(hidden).astype(BF16).reshape(views, padded, hid.shape[2])
    for i in range(views):
        raw = lax.dot_general(
            wp[...], hid[i], (((1,), (1,)), ((), ())), preferred_element_type=F32
        )
        conf = 1.0 + jnp.exp(raw[3:4])
        last = lax.broadcasted_iota(jnp.int32, raw.shape, 0) == 3
        contrib = jnp.where(last, conf, raw * conf)
        image = table[2, i]
        out[image] = out[image] + contrib[:, :tokens]


def per_device(
    tokens,
    gain_query,
    gain_context,
    query_weight,
    key_weight,
    value_weight,
    out_weight,
    gain_head,
    hidden_weight,
    hidden_bias,
    point_weight,
    view_owner,
    view_local,
    pair_count,
):
    worker_count = lax.axis_size("pairs")
    core_count = lax.axis_size("mp")
    worker = lax.axis_index("pairs").astype(jnp.int32)
    core = lax.axis_index("mp").astype(jnp.int32)
    image_count, token_count, half = tokens.shape
    width, hidden_width = hidden_weight.shape
    rows = -(-token_count // 8) * 8
    padded = -(-token_count // 16) * 16
    views = 3

    shard = jnp.pad(tokens, ((0, 0), (0, rows - token_count), (0, 0)))
    parts = ring_gather(shard, worker_count)
    table = plan(
        view_owner[:, 0], view_local, pair_count, worker, core, image_count, worker_count
    )

    count = len(parts)
    anywhere = pl.BlockSpec(memory_space=pl.ANY)
    scalars = pl.BlockSpec(memory_space=pltpu.SMEM)
    vector = pl.BlockSpec(memory_space=pltpu.VMEM)
    send = pl.pallas_call(
        functools.partial(pick_kernel, count),
        out_shape=jax.ShapeDtypeStruct((4, rows, half), BF16),
        in_specs=[scalars] + [anywhere] * count,
        out_specs=anywhere,
        scratch_shapes=[pltpu.SemaphoreType.DMA((4,))],
        name="pick",
    )(table, *parts)
    other = lax.ppermute(send, "mp", [(0, 1), (1, 0)])

    flat = pl.pallas_call(
        functools.partial(decode_kernel, count, token_count),
        out_shape=jax.ShapeDtypeStruct((worker_count * image_count, 4, token_count), F32),
        in_specs=[scalars] + [anywhere] * (count + 1) + [vector] * 5 + [anywhere] * 5,
        out_specs=vector,
        scratch_shapes=[
            pltpu.VMEM((4, rows, half), BF16),
            pltpu.VMEM((4, rows, half), BF16),
            pltpu.VMEM((views, padded, width), BF16),
            pltpu.VMEM((views, padded, width), BF16),
            pltpu.VMEM((views, padded, width), BF16),
            pltpu.VMEM((views, padded, width), BF16),
            pltpu.VMEM((views, padded, width), BF16),
            pltpu.VMEM((views, padded, width), BF16),
            pltpu.VMEM((views, padded, width), BF16),
            pltpu.VMEM((views, padded, hidden_width), BF16),
            pltpu.VMEM((width, width), BF16),
            pltpu.VMEM((width, width), BF16),
            pltpu.VMEM((width, width), BF16),
            pltpu.VMEM((width, width), BF16),
            pltpu.VMEM((width, hidden_width), BF16),
            pltpu.SemaphoreType.DMA((4,)),
            pltpu.SemaphoreType.DMA((5,)),
            pltpu.SemaphoreType.DMA,
        ],
        compiler_params=pltpu.CompilerParams(vmem_limit_bytes=48 * 1024 * 1024),
        name="decode",
    )(
        table,
        *parts,
        other,
        gain_query.reshape(1, width),
        gain_context.reshape(1, width),
        gain_head.reshape(1, width),
        hidden_bias.reshape(1, hidden_width),
        point_weight,
        query_weight,
        key_weight,
        value_weight,
        out_weight,
        hidden_weight,
    )
    arrived = lax.all_to_all(flat, ("pairs", "mp"), 0, 0, tiled=True)
    mine = image_count // core_count
    return jnp.sum(arrived.reshape(worker_count * core_count, mine, 4, token_count), axis=0)


def solution(mesh):
    return jax.shard_map(
        per_device,
        mesh=mesh,
        in_specs=(
            P(("groups", "pairs"), None, "mp"),
            P(),
            P(),
            P(),
            P(),
            P(),
            P(),
            P(),
            P(),
            P(),
            P(),
            P("groups", None),
            P("groups"),
            P("groups"),
        ),
        out_specs=P(("groups", "pairs", "mp"), None, None),
        check_vma=False,
    )
```

```python
import functools

import jax
import jax.numpy as jnp
from jax import lax
from jax.experimental import pallas as pl
from jax.experimental.pallas import tpu as pltpu
from jax.sharding import PartitionSpec as P

HEADS = 12
EPS = 1e-06
F32 = jnp.float32
BF16 = jnp.bfloat16


def in_hbm(array):
    return pltpu.with_memory_space_constraint(array, pltpu.HBM)


def in_vmem(array):
    return pltpu.with_memory_space_constraint(array, pltpu.VMEM)


def ring_place(index, count):
    if count > 8:
        return index
    half = index // 2
    return jnp.where(index % 2 == 0, half, count - 1 - half)


def ring_order(count):
    if count > 8:
        return list(range(count))
    return list(range(0, count, 2)) + list(range(count - 1, 0, -2))


def ring_steps(worker_count):
    order = ring_order(worker_count)
    ahead = [(order[i], order[(i + 1) % worker_count]) for i in range(worker_count)]
    return ahead, [(b, a) for a, b in ahead]


def ring_near(shard, worker_count, reach):
    ahead, back = ring_steps(worker_count)
    parts = {0: shard}
    going, coming = shard, shard
    for step in range(1, reach + 1):
        going = lax.ppermute(going, "pairs", ahead)
        coming = lax.ppermute(coming, "pairs", back)
        parts[worker_count - step] = going
        parts[step] = coming
    return parts


def ring_far(parts, worker_count, reach):
    ahead, back = ring_steps(worker_count)
    middle = worker_count // 2
    parts = dict(parts)
    going, coming = parts[worker_count - reach], parts[reach]
    half = going.shape[0] // 2
    for step in range(reach + 1, middle):
        going = lax.ppermute(going, "pairs", ahead)
        coming = lax.ppermute(coming, "pairs", back)
        parts[worker_count - step] = going
        parts[step] = coming
    parts[middle] = lax.ppermute(going[:half], "pairs", ahead)
    parts[worker_count] = lax.ppermute(coming[half:], "pairs", back)
    return parts


FIRST = (0, 1, 2, 3, 4, 5, 3, 2)
SECOND = (4, 5, 3, 2, 0, 1, 2, 3)


def deal_kernel(
    worker_count,
    image_count,
    reach,
    owners,
    locals_,
    counts,
    me,
    table,
    first,
    fits,
    holder,
    spot,
    load,
    members,
    parent,
):
    share = 3
    requests = owners.shape[0] // worker_count
    pairs = worker_count * share
    everyone = 2**worker_count - 1

    def list_worker(w, r):
        def list_slot(s, r):
            first[r] = w * requests + 2 * s
            return r + 1

        return lax.fori_loop(0, counts[w], list_slot, r)

    lax.fori_loop(0, worker_count, list_worker, 0)

    def near(view):
        place = ring_place(owners[view], worker_count)
        turned = (2 ** (2 * reach + 1) - 1) << lax.rem(place + worker_count - reach, worker_count)
        return (turned | (turned >> worker_count)) & everyone

    def set_pair(r, carry):
        fits[r] = near(first[r]) & near(first[r] + 1)
        holder[r] = -1
        spot[r] = 0
        return carry

    lax.fori_loop(0, pairs, set_pair, 0)
    for w in range(worker_count):
        load[w] = 0

    def put(pair, w, slot):
        members[w * share + slot] = pair
        holder[pair] = w
        spot[pair] = slot

    def match(r, missed):
        for w in range(worker_count):
            parent[w] = r

        def searching(state):
            seen, done, found = state
            return jnp.logical_and(found < 0, (seen & ~done) != 0)

        def search(state):
            seen, done, found = state
            todo = seen & ~done
            w = jnp.int32(0)
            for x in range(worker_count - 1, -1, -1):
                w = jnp.where(((todo >> x) & 1) == 1, jnp.int32(x), w)
            room = load[w] < share
            fresh_all = jnp.int32(0)
            for i in range(share):
                q = jnp.where(room, r, members[w * share + i])
                fresh = jnp.where(room, 0, fits[q] & ~(seen | fresh_all))
                for x in range(worker_count):

                    @pl.when(((fresh >> x) & 1) == 1)
                    def _():
                        parent[x] = q

                fresh_all = fresh_all | fresh
            return seen | fresh_all, done | (1 << w), jnp.where(room, w, found)

        start = (fits[r], jnp.int32(0), jnp.int32(-1))
        _, _, found = lax.while_loop(searching, search, start)

        @pl.when(found >= 0)
        def _():
            def moving(state):
                return state[0] >= 0

            def move(state):
                w, slot = state
                pair = parent[w]
                after = (holder[pair], spot[pair])
                put(pair, w, slot)
                return after

            slot = load[found]
            load[found] = slot + 1
            lax.while_loop(moving, move, (found, slot))

        return missed + jnp.where(found < 0, 1, 0)

    for w in range(pairs):
        members[w] = 0
    missed = lax.fori_loop(0, pairs, match, jnp.int32(0))

    @pl.when(missed > 0)
    def _():
        def place_pair(r, carry):
            def try_worker(w, carry):
                @pl.when(jnp.logical_and(holder[r] < 0, load[w] < share))
                def _():
                    put(r, w, load[w])
                    load[w] = load[w] + 1

                return carry

            return lax.fori_loop(0, worker_count, try_worker, carry)

        lax.fori_loop(0, pairs, place_pair, 0)

    core = me[1]
    here = ring_place(me[0], worker_count)
    middle, half = worker_count // 2, image_count // 2
    for column in range(8):
        place = jnp.where(core == 0, FIRST[column], SECOND[column])
        view = first[members[here * share + place // 2]] + lax.rem(place, 2)
        owner, row = owners[view], locals_[view]
        gap = lax.rem(ring_place(owner, worker_count) - here + worker_count, worker_count)
        late = jnp.logical_and(gap == middle, row >= half)
        table[0, column] = jnp.where(late, worker_count, gap)
        table[1, column] = jnp.where(late, row - half, row)
        table[2, column] = owner * image_count + row
        table[3, column] = core
        table[4, column] = jnp.where(missed == 0, 1, 0)


def plan(owners, locals_, counts, worker, core, image_count, worker_count):
    requests = locals_.shape[0] // worker_count
    share = requests // 4
    place = jnp.where(core == 0, jnp.array(FIRST, jnp.int32), jnp.array(SECOND, jnp.int32))
    pair = worker * share + place // 2
    workers = jnp.arange(worker_count, dtype=jnp.int32)
    upto = jnp.sum(
        jnp.where(workers[None, :] <= workers[:, None], counts[None, :], 0), axis=1
    )
    past = upto[None, :] <= pair[:, None]
    holder = jnp.sum(past.astype(jnp.int32), axis=1)
    slot = pair - jnp.sum(jnp.where(past, counts[None, :], 0), axis=1)
    view = holder * requests + slot * 2 + place % 2
    all_images = owners * image_count + locals_
    ids = jnp.arange(all_images.shape[0], dtype=jnp.int32)
    image = jnp.sum(jnp.where(view[:, None] == ids[None, :], all_images[None, :], 0), axis=1)
    owner, row = image // image_count, image % image_count
    gap = (ring_place(owner, worker_count) - ring_place(worker, worker_count)) % worker_count
    middle, half = worker_count // 2, image_count // 2
    late = jnp.logical_and(gap == middle, row >= half)
    part = jnp.where(late, worker_count, gap)
    row = jnp.where(late, row - half, row)
    head = jnp.broadcast_to(jnp.asarray(core, jnp.int32), (8,))
    return jnp.stack([part, row, image, head])


def fetch(table, column, keys, parts, target, sem, wait):
    if wait:
        pltpu.make_async_copy(parts[0].at[0], target, sem).wait()
        return
    part, row = table[0, column], table[1, column]
    for key, source in zip(keys, parts, strict=True):

        @pl.when(part == key)
        def _():
            pltpu.make_async_copy(source.at[row], target, sem).start()


def pick_kernel(keys, table, *refs):
    parts, (keep, send, sems) = refs[: len(keys)], refs[len(keys) :]
    for wait in (False, True):
        for j in range(4):
            fetch(table, 4 + j, keys, parts, send.at[j], sems.at[4 + j], wait)
            fetch(table, j, keys, parts, keep.at[j], sems.at[j], wait)


def pick(table, parts):
    keys = sorted(parts)
    hold = in_vmem if len(keys) < 10 else in_hbm
    space = pltpu.VMEM if len(keys) < 10 else pltpu.HBM
    _, rows, half = parts[0].shape
    picked = jax.ShapeDtypeStruct((4, rows, half), BF16)
    vector = pl.BlockSpec(memory_space=pltpu.VMEM)
    return pl.pallas_call(
        functools.partial(pick_kernel, keys),
        out_shape=(picked, picked),
        in_specs=[pl.BlockSpec(memory_space=pltpu.SMEM)]
        + [pl.BlockSpec(memory_space=space)] * len(keys),
        out_specs=(vector, vector),
        scratch_shapes=[pltpu.SemaphoreType.DMA((8,))],
        compiler_params=pltpu.CompilerParams(vmem_limit_bytes=8 * 1024 * 1024),
        name="pick",
    )(table, *[hold(parts[key]) for key in keys])


def norm_last(rows, gain):
    average = jnp.mean(rows, axis=-1, keepdims=True)
    centered = rows - average
    variance = jnp.mean(centered * centered, axis=-1, keepdims=True)
    return centered * lax.rsqrt(variance + EPS) * gain


def decode_kernel(tokens, table, *refs):
    (mine, theirs, gain_q, gain_c, gain_h, bias_h, wp) = refs[:7]
    weights, out = refs[7:12], refs[12]
    (xq, xc, res, q, k, v, att, hid) = refs[13:21]
    held, wsems = refs[21:26], refs[26]
    wq, wk, wv, wo, wh = held
    rows, half = mine.shape[1], mine.shape[2]
    views, padded, width = q.shape
    core = table[3, 0]

    copies = [
        pltpu.make_async_copy(weights[i], held[i], wsems.at[i]) for i in range(len(weights))
    ]
    for copy in copies:
        copy.start()

    out[...] = jnp.zeros_like(out)
    tail = jnp.zeros((views, padded - rows, width), BF16)
    xq[:, rows:, :] = tail
    xc[:, rows:, :] = tail
    res[:, rows:, :] = tail

    here = pl.ds(pl.multiple_of(core * half, half), half)
    there = pl.ds(pl.multiple_of((1 - core) * half, half), half)
    context_of = (1, 0, None, 2)
    for j in range(4):
        raw_a, raw_b = mine[j], theirs[j]
        a, b = raw_a.astype(F32), raw_b.astype(F32)
        average = (
            jnp.sum(a, axis=-1, keepdims=True) + jnp.sum(b, axis=-1, keepdims=True)
        ) / width
        a, b = a - average, b - average
        variance = (
            jnp.sum(a * a, axis=-1, keepdims=True) + jnp.sum(b * b, axis=-1, keepdims=True)
        ) / width
        scale = lax.rsqrt(variance + EPS)
        a, b = a * scale, b * scale
        if j < views:
            xq[j, :rows, here] = (a * gain_q[:, here]).astype(BF16)
            xq[j, :rows, there] = (b * gain_q[:, there]).astype(BF16)
            res[j, :rows, here] = raw_a
            res[j, :rows, there] = raw_b
        if context_of[j] is not None:
            xc[context_of[j], :rows, here] = (a * gain_c[:, here]).astype(BF16)
            xc[context_of[j], :rows, there] = (b * gain_c[:, there]).astype(BF16)

    total = views * padded
    head_size = width // HEADS
    queries = xq[...].reshape(total, width)
    contexts = xc[...].reshape(total, width)
    copies[0].wait()
    proj = jnp.dot(queries, wq[...], preferred_element_type=F32)
    q[...] = (proj.astype(BF16) * BF16(head_size**-0.5)).reshape(views, padded, width)
    copies[1].wait()
    proj = jnp.dot(contexts, wk[...], preferred_element_type=F32)
    k[...] = proj.astype(BF16).reshape(views, padded, width)
    copies[2].wait()
    proj = jnp.dot(contexts, wv[...], preferred_element_type=F32)
    v[...] = proj.astype(BF16).reshape(views, padded, width)

    block = 2 * head_size
    low = lax.broadcasted_iota(jnp.int32, (padded, block), 1) < head_size
    hide = jnp.where(lax.broadcasted_iota(jnp.int32, (1, padded), 1) < tokens, 0.0, -1e30)
    nothing = jnp.zeros((padded, block), BF16)

    def attend(i, carry):
        for b in range(width // block):
            cols = slice(b * block, (b + 1) * block)
            qb, kb, vb = q[i, :, cols], k[i, :, cols], v[i, :, cols]
            blended = []
            for keep in (0, 1):
                qh = jnp.where(low, qb, nothing) if keep == 0 else jnp.where(low, nothing, qb)
                scores = lax.dot_general(
                    qh, kb, (((1,), (1,)), ((), ())), preferred_element_type=F32
                )
                scores = scores + hide
                peak = jnp.max(scores, axis=-1, keepdims=True)
                expo = jnp.exp(scores - peak)
                inverse = 1.0 / jnp.sum(expo, axis=-1, keepdims=True)
                probs = (expo * inverse).astype(BF16)
                blended.append(jnp.dot(probs, vb, preferred_element_type=F32))
            att[i, :, cols] = jnp.where(low, blended[0], blended[1]).astype(BF16)
        return carry

    lax.fori_loop(0, views, attend, 0)

    copies[3].wait()
    updated = jnp.dot(att[...].reshape(total, width), wo[...], preferred_element_type=F32)
    updated = updated + res[...].reshape(total, width).astype(F32)
    head_in = norm_last(updated, gain_h[...]).astype(BF16)
    copies[4].wait()
    hidden = jnp.dot(head_in, wh[...], preferred_element_type=F32) + bias_h[...]
    hid[...] = jax.nn.gelu(hidden).astype(BF16).reshape(views, padded, hid.shape[2])
    for i in range(views):
        raw = lax.dot_general(
            wp[...], hid[i], (((1,), (1,)), ((), ())), preferred_element_type=F32
        )
        conf = 1.0 + jnp.exp(raw[3:4])
        last = lax.broadcasted_iota(jnp.int32, raw.shape, 0) == 3
        contrib = jnp.where(last, conf, raw * conf)
        image = table[2, i]
        out[image] = out[image] + contrib[:, :tokens]


def per_device(
    tokens,
    gain_query,
    gain_context,
    query_weight,
    key_weight,
    value_weight,
    out_weight,
    gain_head,
    hidden_weight,
    hidden_bias,
    point_weight,
    view_owner,
    view_local,
    pair_count,
):
    worker_count = lax.axis_size("pairs")
    core_count = lax.axis_size("mp")
    worker = lax.axis_index("pairs").astype(jnp.int32)
    core = lax.axis_index("mp").astype(jnp.int32)
    image_count, token_count, half = tokens.shape
    width, hidden_width = hidden_weight.shape
    rows = -(-token_count // 8) * 8
    padded = -(-token_count // 16) * 16
    views = 3

    shard = jnp.pad(tokens, ((0, 0), (0, rows - token_count), (0, 0)))
    anywhere = pl.BlockSpec(memory_space=pltpu.HBM)
    scalars = pl.BlockSpec(memory_space=pltpu.SMEM)
    vector = pl.BlockSpec(memory_space=pltpu.VMEM)
    owners = view_owner[:, 0]
    if worker_count == 8:
        reach = 2
        pairs = worker_count * views
        table = pl.pallas_call(
            functools.partial(deal_kernel, worker_count, image_count, reach),
            out_shape=jax.ShapeDtypeStruct((5, 8), jnp.int32),
            in_specs=[scalars] * 4,
            out_specs=scalars,
            scratch_shapes=[pltpu.SMEM((pairs,), jnp.int32)] * 4
            + [pltpu.SMEM((worker_count,), jnp.int32), pltpu.SMEM((pairs,), jnp.int32)]
            + [pltpu.SMEM((worker_count,), jnp.int32)],
            compiler_params=pltpu.CompilerParams(vmem_limit_bytes=2 * 1024 * 1024),
            name="deal",
        )(owners, view_local, pair_count, jnp.stack([worker, core]))
        parts = ring_near(shard, worker_count, reach)
        keep, send = lax.cond(
            table[4, 0] == 1,
            lambda near: pick(table, near),
            lambda near: pick(table, ring_far(near, worker_count, reach)),
            parts,
        )
    else:
        table = plan(owners, view_local, pair_count, worker, core, image_count, worker_count)
        parts = ring_far({0: shard, worker_count: shard}, worker_count, 0)
        keep, send = pick(table, parts)
    other = lax.ppermute(send, "mp", [(0, 1), (1, 0)])

    wide = pltpu.VMEM((views, padded, width), BF16)
    square = pltpu.VMEM((width, width), BF16)
    flat = pl.pallas_call(
        functools.partial(decode_kernel, token_count),
        out_shape=jax.ShapeDtypeStruct((worker_count * image_count, 4, token_count), F32),
        in_specs=[scalars] + [vector] * 7 + [anywhere] * 5,
        out_specs=vector,
        scratch_shapes=[wide] * 7
        + [pltpu.VMEM((views, padded, hidden_width), BF16)]
        + [square] * 4
        + [pltpu.VMEM((width, hidden_width), BF16), pltpu.SemaphoreType.DMA((5,))],
        compiler_params=pltpu.CompilerParams(vmem_limit_bytes=32 * 1024 * 1024),
        name="decode",
    )(
        table,
        keep,
        other,
        gain_query.reshape(1, width),
        gain_context.reshape(1, width),
        gain_head.reshape(1, width),
        hidden_bias.reshape(1, hidden_width),
        point_weight,
        in_hbm(query_weight),
        in_hbm(key_weight),
        in_hbm(value_weight),
        in_hbm(out_weight),
        in_hbm(hidden_weight),
    )
    arrived = lax.all_to_all(flat, ("pairs", "mp"), 0, 0, tiled=True)
    mine = image_count // core_count
    return jnp.sum(arrived.reshape(worker_count * core_count, mine, 4, token_count), axis=0)


def solution(mesh):
    return jax.shard_map(
        per_device,
        mesh=mesh,
        in_specs=(
            P(("groups", "pairs"), None, "mp"),
            P(),
            P(),
            P(),
            P(),
            P(),
            P(),
            P(),
            P(),
            P(),
            P(),
            P("groups", None),
            P("groups"),
            P("groups"),
        ),
        out_specs=P(("groups", "pairs", "mp"), None, None),
        check_vma=False,
    )
```

```python
import functools

import jax
import jax.numpy as jnp
from jax import lax
from jax.experimental import pallas as pl
from jax.experimental.pallas import tpu as pltpu
from jax.sharding import PartitionSpec as P

HEADS = 12
EPS = 1e-06
F32 = jnp.float32
BF16 = jnp.bfloat16


def in_hbm(array):
    return pltpu.with_memory_space_constraint(array, pltpu.HBM)


def in_vmem(array):
    return pltpu.with_memory_space_constraint(array, pltpu.VMEM)


def ring_place(index, count):
    if count > 8:
        return index
    half = index // 2
    return jnp.where(index % 2 == 0, half, count - 1 - half)


def ring_order(count):
    if count > 8:
        return list(range(count))
    return list(range(0, count, 2)) + list(range(count - 1, 0, -2))


def ring_steps(worker_count):
    order = ring_order(worker_count)
    ahead = [(order[i], order[(i + 1) % worker_count]) for i in range(worker_count)]
    return ahead, [(b, a) for a, b in ahead]


def ring_near(shard, worker_count, reach):
    ahead, back = ring_steps(worker_count)
    parts = {0: shard}
    going, coming = shard, shard
    for step in range(1, reach + 1):
        going = lax.ppermute(going, "pairs", ahead)
        coming = lax.ppermute(coming, "pairs", back)
        parts[worker_count - step] = going
        parts[step] = coming
    return parts


def ring_far(parts, worker_count, reach):
    ahead, back = ring_steps(worker_count)
    middle = worker_count // 2
    parts = dict(parts)
    going, coming = parts[worker_count - reach], parts[reach]
    half = going.shape[0] // 2
    for step in range(reach + 1, middle):
        going = lax.ppermute(going, "pairs", ahead)
        coming = lax.ppermute(coming, "pairs", back)
        parts[worker_count - step] = going
        parts[step] = coming
    parts[middle] = lax.ppermute(going[:half], "pairs", ahead)
    parts[worker_count] = lax.ppermute(coming[half:], "pairs", back)
    return parts


FIRST = (0, 1, 2, 3, 4, 5, 3, 2)
SECOND = (4, 5, 3, 2, 0, 1, 2, 3)


def deal_kernel(
    worker_count,
    image_count,
    reach,
    owners,
    locals_,
    counts,
    me,
    table,
    first,
    fits,
    holder,
    spot,
    load,
    members,
    parent,
):
    share = 3
    requests = owners.shape[0] // worker_count
    pairs = worker_count * share
    everyone = 2**worker_count - 1

    def list_worker(w, r):
        def list_slot(s, r):
            first[r] = w * requests + 2 * s
            return r + 1

        return lax.fori_loop(0, counts[w], list_slot, r)

    lax.fori_loop(0, worker_count, list_worker, 0)

    def near(view):
        place = ring_place(owners[view], worker_count)
        turned = (2 ** (2 * reach + 1) - 1) << lax.rem(place + worker_count - reach, worker_count)
        return (turned | (turned >> worker_count)) & everyone

    def set_pair(r, carry):
        fits[r] = near(first[r]) & near(first[r] + 1)
        holder[r] = -1
        spot[r] = 0
        return carry

    lax.fori_loop(0, pairs, set_pair, 0)
    for w in range(worker_count):
        load[w] = 0

    def put(pair, w, slot):
        members[w * share + slot] = pair
        holder[pair] = w
        spot[pair] = slot

    def match(r, missed):
        for w in range(worker_count):
            parent[w] = r

        def searching(state):
            seen, done, found = state
            return jnp.logical_and(found < 0, (seen & ~done) != 0)

        def search(state):
            seen, done, found = state
            todo = seen & ~done
            w = jnp.int32(0)
            for x in range(worker_count - 1, -1, -1):
                w = jnp.where(((todo >> x) & 1) == 1, jnp.int32(x), w)
            room = load[w] < share
            fresh_all = jnp.int32(0)
            for i in range(share):
                q = jnp.where(room, r, members[w * share + i])
                fresh = jnp.where(room, 0, fits[q] & ~(seen | fresh_all))
                for x in range(worker_count):

                    @pl.when(((fresh >> x) & 1) == 1)
                    def _():
                        parent[x] = q

                fresh_all = fresh_all | fresh
            return seen | fresh_all, done | (1 << w), jnp.where(room, w, found)

        start = (fits[r], jnp.int32(0), jnp.int32(-1))
        _, _, found = lax.while_loop(searching, search, start)

        @pl.when(found >= 0)
        def _():
            def moving(state):
                return state[0] >= 0

            def move(state):
                w, slot = state
                pair = parent[w]
                after = (holder[pair], spot[pair])
                put(pair, w, slot)
                return after

            slot = load[found]
            load[found] = slot + 1
            lax.while_loop(moving, move, (found, slot))

        return missed + jnp.where(found < 0, 1, 0)

    for w in range(pairs):
        members[w] = 0
    missed = lax.fori_loop(0, pairs, match, jnp.int32(0))

    @pl.when(missed > 0)
    def _():
        def place_pair(r, carry):
            def try_worker(w, carry):
                @pl.when(jnp.logical_and(holder[r] < 0, load[w] < share))
                def _():
                    put(r, w, load[w])
                    load[w] = load[w] + 1

                return carry

            return lax.fori_loop(0, worker_count, try_worker, carry)

        lax.fori_loop(0, pairs, place_pair, 0)

    core = me[1]
    here = ring_place(me[0], worker_count)
    middle, half = worker_count // 2, image_count // 2
    for column in range(8):
        place = jnp.where(core == 0, FIRST[column], SECOND[column])
        view = first[members[here * share + place // 2]] + lax.rem(place, 2)
        owner, row = owners[view], locals_[view]
        gap = lax.rem(ring_place(owner, worker_count) - here + worker_count, worker_count)
        late = jnp.logical_and(gap == middle, row >= half)
        table[0, column] = jnp.where(late, worker_count, gap)
        table[1, column] = jnp.where(late, row - half, row)
        table[2, column] = owner * image_count + row
        table[3, column] = core
        table[4, column] = jnp.where(missed == 0, 1, 0)


def plan(owners, locals_, counts, worker, core, image_count, worker_count):
    requests = locals_.shape[0] // worker_count
    share = requests // 4
    place = jnp.where(core == 0, jnp.array(FIRST, jnp.int32), jnp.array(SECOND, jnp.int32))
    pair = worker * share + place // 2
    workers = jnp.arange(worker_count, dtype=jnp.int32)
    upto = jnp.sum(
        jnp.where(workers[None, :] <= workers[:, None], counts[None, :], 0), axis=1
    )
    past = upto[None, :] <= pair[:, None]
    holder = jnp.sum(past.astype(jnp.int32), axis=1)
    slot = pair - jnp.sum(jnp.where(past, counts[None, :], 0), axis=1)
    view = holder * requests + slot * 2 + place % 2
    all_images = owners * image_count + locals_
    ids = jnp.arange(all_images.shape[0], dtype=jnp.int32)
    image = jnp.sum(jnp.where(view[:, None] == ids[None, :], all_images[None, :], 0), axis=1)
    owner, row = image // image_count, image % image_count
    gap = (ring_place(owner, worker_count) - ring_place(worker, worker_count)) % worker_count
    middle, half = worker_count // 2, image_count // 2
    late = jnp.logical_and(gap == middle, row >= half)
    part = jnp.where(late, worker_count, gap)
    row = jnp.where(late, row - half, row)
    head = jnp.broadcast_to(jnp.asarray(core, jnp.int32), (8,))
    return jnp.stack([part, row, image, head])


def fetch(table, column, keys, parts, target, sem, wait):
    if wait:
        pltpu.make_async_copy(parts[0].at[0], target, sem).wait()
        return
    part, row = table[0, column], table[1, column]
    for key, source in zip(keys, parts, strict=True):

        @pl.when(part == key)
        def _():
            pltpu.make_async_copy(source.at[row], target, sem).start()


def pick_kernel(keys, first_column, table, *refs):
    parts, (out, sems) = refs[: len(keys)], refs[-2:]
    for wait in (False, True):
        for j in range(4):
            fetch(table, first_column + j, keys, parts, out.at[j], sems.at[j], wait)


def pick(table, parts, first_column, held):
    keys = sorted(parts)
    hold = in_vmem if len(keys) < 10 else in_hbm
    space = pltpu.VMEM if len(keys) < 10 else pltpu.HBM
    _, rows, half = parts[0].shape
    return pl.pallas_call(
        functools.partial(pick_kernel, keys, first_column),
        out_shape=jax.ShapeDtypeStruct((4, rows, half), BF16),
        in_specs=[pl.BlockSpec(memory_space=pltpu.SMEM)]
        + [pl.BlockSpec(memory_space=space)] * len(keys)
        + [pl.BlockSpec(memory_space=pltpu.VMEM)] * len(held),
        out_specs=pl.BlockSpec(memory_space=pltpu.VMEM),
        scratch_shapes=[pltpu.SemaphoreType.DMA((4,))],
        compiler_params=pltpu.CompilerParams(vmem_limit_bytes=8 * 1024 * 1024),
        cost_estimate=pl.CostEstimate(
            flops=0, bytes_accessed=16 * rows * half, transcendentals=0
        ),
        name="pick",
    )(table, *[hold(parts[key]) for key in keys], *[in_vmem(array) for array in held])


def stage_kernel(count, *refs):
    sources, targets, sems = refs[:count], refs[count : 2 * count], refs[2 * count]
    copies = [pltpu.make_async_copy(sources[i], targets[i], sems.at[i]) for i in range(count)]
    for copy in copies:
        copy.start()
    for copy in copies:
        copy.wait()


def stage(arrays):
    count = len(arrays)
    size = sum(array.size * array.dtype.itemsize for array in arrays)
    return pl.pallas_call(
        functools.partial(stage_kernel, count),
        out_shape=tuple(jax.ShapeDtypeStruct(array.shape, array.dtype) for array in arrays),
        in_specs=[pl.BlockSpec(memory_space=pltpu.HBM)] * count,
        out_specs=(pl.BlockSpec(memory_space=pltpu.VMEM),) * count,
        scratch_shapes=[pltpu.SemaphoreType.DMA((count,))],
        compiler_params=pltpu.CompilerParams(vmem_limit_bytes=16 * 1024 * 1024),
        cost_estimate=pl.CostEstimate(flops=0, bytes_accessed=2 * size, transcendentals=0),
        name="stage",
    )(*[in_hbm(array) for array in arrays])


def gather_images(table, parts, held):
    other = lax.ppermute(pick(table, parts, 4, held), "mp", [(0, 1), (1, 0)])
    return pick(table, parts, 0, held), other


def norm_last(rows, gain):
    average = jnp.mean(rows, axis=-1, keepdims=True)
    centered = rows - average
    variance = jnp.mean(centered * centered, axis=-1, keepdims=True)
    return centered * lax.rsqrt(variance + EPS) * gain


def decode_kernel(tokens, table, *refs):
    (mine, theirs, gain_q, gain_c, gain_h, bias_h, wp) = refs[:7]
    wq, wk, wv, wo, wh = refs[7:12]
    out = refs[12]
    (xq, xc, res, q, k, v, att, hid) = refs[13:]
    rows, half = mine.shape[1], mine.shape[2]
    views, padded, width = q.shape
    core = table[3, 0]

    out[...] = jnp.zeros_like(out)
    tail = jnp.zeros((views, padded - rows, width), BF16)
    xq[:, rows:, :] = tail
    xc[:, rows:, :] = tail
    res[:, rows:, :] = tail

    here = pl.ds(pl.multiple_of(core * half, half), half)
    there = pl.ds(pl.multiple_of((1 - core) * half, half), half)
    context_of = (1, 0, None, 2)
    for j in range(4):
        raw_a, raw_b = mine[j], theirs[j]
        a, b = raw_a.astype(F32), raw_b.astype(F32)
        average = (
            jnp.sum(a, axis=-1, keepdims=True) + jnp.sum(b, axis=-1, keepdims=True)
        ) / width
        a, b = a - average, b - average
        variance = (
            jnp.sum(a * a, axis=-1, keepdims=True) + jnp.sum(b * b, axis=-1, keepdims=True)
        ) / width
        scale = lax.rsqrt(variance + EPS)
        a, b = a * scale, b * scale
        if j < views:
            xq[j, :rows, here] = (a * gain_q[:, here]).astype(BF16)
            xq[j, :rows, there] = (b * gain_q[:, there]).astype(BF16)
            res[j, :rows, here] = raw_a
            res[j, :rows, there] = raw_b
        if context_of[j] is not None:
            xc[context_of[j], :rows, here] = (a * gain_c[:, here]).astype(BF16)
            xc[context_of[j], :rows, there] = (b * gain_c[:, there]).astype(BF16)

    total = views * padded
    head_size = width // HEADS
    queries = xq[...].reshape(total, width)
    contexts = xc[...].reshape(total, width)
    proj = jnp.dot(queries, wq[...], preferred_element_type=F32)
    q[...] = (proj.astype(BF16) * BF16(head_size**-0.5)).reshape(views, padded, width)
    proj = jnp.dot(contexts, wk[...], preferred_element_type=F32)
    k[...] = proj.astype(BF16).reshape(views, padded, width)
    proj = jnp.dot(contexts, wv[...], preferred_element_type=F32)
    v[...] = proj.astype(BF16).reshape(views, padded, width)

    block = 2 * head_size
    low = lax.broadcasted_iota(jnp.int32, (padded, block), 1) < head_size
    hide = jnp.where(lax.broadcasted_iota(jnp.int32, (1, padded), 1) < tokens, 0.0, -1e30)
    nothing = jnp.zeros((padded, block), BF16)

    def attend(i, carry):
        for b in range(width // block):
            cols = slice(b * block, (b + 1) * block)
            qb, kb, vb = q[i, :, cols], k[i, :, cols], v[i, :, cols]
            blended = []
            for keep in (0, 1):
                qh = jnp.where(low, qb, nothing) if keep == 0 else jnp.where(low, nothing, qb)
                scores = lax.dot_general(
                    qh, kb, (((1,), (1,)), ((), ())), preferred_element_type=F32
                )
                scores = scores + hide
                peak = jnp.max(scores, axis=-1, keepdims=True)
                expo = jnp.exp(scores - peak)
                inverse = 1.0 / jnp.sum(expo, axis=-1, keepdims=True)
                probs = (expo * inverse).astype(BF16)
                blended.append(jnp.dot(probs, vb, preferred_element_type=F32))
            att[i, :, cols] = jnp.where(low, blended[0], blended[1]).astype(BF16)
        return carry

    lax.fori_loop(0, views, attend, 0)

    updated = jnp.dot(att[...].reshape(total, width), wo[...], preferred_element_type=F32)
    updated = updated + res[...].reshape(total, width).astype(F32)
    head_in = norm_last(updated, gain_h[...]).astype(BF16)
    hidden = jnp.dot(head_in, wh[...], preferred_element_type=F32) + bias_h[...]
    hid[...] = jax.nn.gelu(hidden).astype(BF16).reshape(views, padded, hid.shape[2])
    for i in range(views):
        raw = lax.dot_general(
            wp[...], hid[i], (((1,), (1,)), ((), ())), preferred_element_type=F32
        )
        conf = 1.0 + jnp.exp(raw[3:4])
        last = lax.broadcasted_iota(jnp.int32, raw.shape, 0) == 3
        contrib = jnp.where(last, conf, raw * conf)
        image = table[2, i]
        out[image] = out[image] + contrib[:, :tokens]


def per_device(
    tokens,
    gain_query,
    gain_context,
    query_weight,
    key_weight,
    value_weight,
    out_weight,
    gain_head,
    hidden_weight,
    hidden_bias,
    point_weight,
    view_owner,
    view_local,
    pair_count,
):
    worker_count = lax.axis_size("pairs")
    core_count = lax.axis_size("mp")
    worker = lax.axis_index("pairs").astype(jnp.int32)
    core = lax.axis_index("mp").astype(jnp.int32)
    image_count, token_count, half = tokens.shape
    width, hidden_width = hidden_weight.shape
    rows = -(-token_count // 8) * 8
    padded = -(-token_count // 16) * 16
    views = 3

    shard = jnp.pad(tokens, ((0, 0), (0, rows - token_count), (0, 0)))
    scalars = pl.BlockSpec(memory_space=pltpu.SMEM)
    vector = pl.BlockSpec(memory_space=pltpu.VMEM)
    owners = view_owner[:, 0]
    weights = stage((query_weight, key_weight, value_weight, out_weight, hidden_weight))
    vectors = (
        gain_query.reshape(1, width),
        gain_context.reshape(1, width),
        gain_head.reshape(1, width),
        hidden_bias.reshape(1, hidden_width),
        point_weight,
    )
    wide = pltpu.VMEM((views, padded, width), BF16)

    def decode(table, parts, vectors, weights):
        keep, other = gather_images(table, parts, weights)
        return pl.pallas_call(
            functools.partial(decode_kernel, token_count),
            out_shape=jax.ShapeDtypeStruct((worker_count * image_count, 4, token_count), F32),
            in_specs=[scalars] + [vector] * 12,
            out_specs=vector,
            scratch_shapes=[wide] * 7 + [pltpu.VMEM((views, padded, hidden_width), BF16)],
            compiler_params=pltpu.CompilerParams(vmem_limit_bytes=32 * 1024 * 1024),
            name="decode",
        )(table, in_vmem(keep), in_vmem(other), *vectors, *[in_vmem(w) for w in weights])

    if worker_count == 8:
        reach = 2
        pairs = worker_count * views
        table = pl.pallas_call(
            functools.partial(deal_kernel, worker_count, image_count, reach),
            out_shape=jax.ShapeDtypeStruct((5, 8), jnp.int32),
            in_specs=[scalars] * 4,
            out_specs=scalars,
            scratch_shapes=[pltpu.SMEM((pairs,), jnp.int32)] * 4
            + [pltpu.SMEM((worker_count,), jnp.int32), pltpu.SMEM((pairs,), jnp.int32)]
            + [pltpu.SMEM((worker_count,), jnp.int32)],
            compiler_params=pltpu.CompilerParams(vmem_limit_bytes=2 * 1024 * 1024),
            cost_estimate=pl.CostEstimate(flops=0, bytes_accessed=20 * 10**6, transcendentals=0),
            name="deal",
        )(owners, view_local, pair_count, jnp.stack([worker, core]))
        parts = ring_near(shard, worker_count, reach)
        flat = lax.cond(
            table[4, 0] == 1,
            decode,
            lambda table, near, *rest: decode(
                table, ring_far(near, worker_count, reach), *rest
            ),
            table,
            parts,
            vectors,
            weights,
        )
    else:
        table = plan(owners, view_local, pair_count, worker, core, image_count, worker_count)
        parts = ring_far({0: shard, worker_count: shard}, worker_count, 0)
        flat = decode(table, parts, vectors, weights)
    arrived = lax.all_to_all(flat, ("pairs", "mp"), 0, 0, tiled=True)
    mine = image_count // core_count
    return jnp.sum(arrived.reshape(worker_count * core_count, mine, 4, token_count), axis=0)


def solution(mesh):
    return jax.shard_map(
        per_device,
        mesh=mesh,
        in_specs=(
            P(("groups", "pairs"), None, "mp"),
            P(),
            P(),
            P(),
            P(),
            P(),
            P(),
            P(),
            P(),
            P(),
            P(),
            P("groups", None),
            P("groups"),
            P("groups"),
        ),
        out_specs=P(("groups", "pairs", "mp"), None, None),
        check_vma=False,
    )
```

```python
import functools

import jax
import jax.numpy as jnp
from jax import lax
from jax.experimental import pallas as pl
from jax.experimental.pallas import tpu as pltpu
from jax.sharding import PartitionSpec as P

HEADS = 12
EPS = 1e-06
F32 = jnp.float32
BF16 = jnp.bfloat16


def in_hbm(array):
    return pltpu.with_memory_space_constraint(array, pltpu.HBM)


def in_vmem(array):
    return pltpu.with_memory_space_constraint(array, pltpu.VMEM)


def ring_place(index, count):
    if count > 8:
        return index
    half = index // 2
    return jnp.where(index % 2 == 0, half, count - 1 - half)


def ring_order(count):
    if count > 8:
        return list(range(count))
    return list(range(0, count, 2)) + list(range(count - 1, 0, -2))


def ring_steps(worker_count):
    order = ring_order(worker_count)
    ahead = [(order[i], order[(i + 1) % worker_count]) for i in range(worker_count)]
    return ahead, [(b, a) for a, b in ahead]


def ring_near(shard, worker_count, reach):
    ahead, back = ring_steps(worker_count)
    parts = {0: shard}
    going, coming = shard, shard
    for step in range(1, reach + 1):
        going = lax.ppermute(going, "pairs", ahead)
        coming = lax.ppermute(coming, "pairs", back)
        parts[worker_count - step] = going
        parts[step] = coming
    return parts


def ring_far(parts, worker_count, reach):
    ahead, back = ring_steps(worker_count)
    middle = worker_count // 2
    parts = dict(parts)
    going, coming = parts[worker_count - reach], parts[reach]
    half = going.shape[0] // 2
    for step in range(reach + 1, middle):
        going = lax.ppermute(going, "pairs", ahead)
        coming = lax.ppermute(coming, "pairs", back)
        parts[worker_count - step] = going
        parts[step] = coming
    parts[middle] = lax.ppermute(going[:half], "pairs", ahead)
    parts[worker_count] = lax.ppermute(coming[half:], "pairs", back)
    return parts


FIRST = (0, 1, 2, 3, 4, 5, 3, 2)
SECOND = (4, 5, 3, 2, 0, 1, 2, 3)
SHARE = 3
MOST = 4
LEVEL = 5


def deal_kernel(
    worker_count,
    image_count,
    reach,
    owners,
    locals_,
    counts,
    me,
    table,
    first,
    fits,
    holder,
    spot,
    load,
    members,
    parent,
):
    requests = owners.shape[0] // worker_count
    pairs = worker_count * SHARE
    everyone = 2**worker_count - 1

    def list_worker(w, r):
        def list_slot(s, r):
            first[r] = w * requests + 2 * s
            return r + 1

        return lax.fori_loop(0, counts[w], list_slot, r)

    lax.fori_loop(0, worker_count, list_worker, 0)

    def near(view):
        place = ring_place(owners[view], worker_count)
        turned = (2 ** (2 * reach + 1) - 1) << lax.rem(place + worker_count - reach, worker_count)
        return (turned | (turned >> worker_count)) & everyone

    def set_pair(r, carry):
        fits[r] = near(first[r]) & near(first[r] + 1)
        holder[r] = -1
        spot[r] = 0
        return carry

    lax.fori_loop(0, pairs, set_pair, 0)
    for w in range(worker_count):
        load[w] = 0
        for x in range(MOST):
            members[w * MOST + x] = 0

    def put(pair, w, slot):
        members[w * MOST + slot] = pair
        holder[pair] = w
        spot[pair] = slot

    def match(most, r):
        for w in range(worker_count):
            parent[w] = r

        def searching(state):
            seen, done, found = state
            return jnp.logical_and(found < 0, (seen & ~done) != 0)

        def search(state):
            seen, done, found = state
            todo = seen & ~done
            w = jnp.int32(0)
            for x in range(worker_count - 1, -1, -1):
                w = jnp.where(((todo >> x) & 1) == 1, jnp.int32(x), w)
            room = load[w] < most
            fresh_all = jnp.int32(0)
            for i in range(most):
                q = jnp.where(room, r, members[w * MOST + i])
                fresh = jnp.where(room, 0, fits[q] & ~(seen | fresh_all))
                for x in range(worker_count):

                    @pl.when(((fresh >> x) & 1) == 1)
                    def _():
                        parent[x] = q

                fresh_all = fresh_all | fresh
            return seen | fresh_all, done | (1 << w), jnp.where(room, w, found)

        start = (fits[r], jnp.int32(0), jnp.int32(-1))
        _, _, found = lax.while_loop(searching, search, start)

        @pl.when(found >= 0)
        def _():
            def moving(state):
                return state[0] >= 0

            def move(state):
                w, slot = state
                pair = parent[w]
                after = (holder[pair], spot[pair])
                put(pair, w, slot)
                return after

            slot = load[found]
            load[found] = slot + 1
            lax.while_loop(moving, move, (found, slot))

        return jnp.where(found < 0, 1, 0)

    missed = lax.fori_loop(0, pairs, lambda r, m: m + match(SHARE, r), jnp.int32(0))
    table[LEVEL, 0] = jnp.where(missed > 0, 1, 0)

    @pl.when(missed > 0)
    def _():
        def again(r, left):
            lost = jnp.where(holder[r] < 0, 1, 0)

            @pl.when(lost == 1)
            def _():
                match(MOST, r)

            return left + jnp.where(holder[r] < 0, 1, 0)

        left = lax.fori_loop(0, pairs, again, jnp.int32(0))

        @pl.when(left > 0)
        def _():
            table[LEVEL, 0] = 2

            def place_pair(r, carry):
                def try_worker(w, carry):
                    @pl.when(jnp.logical_and(holder[r] < 0, load[w] < MOST))
                    def _():
                        put(r, w, load[w])
                        load[w] = load[w] + 1

                    return carry

                return lax.fori_loop(0, worker_count, try_worker, carry)

            lax.fori_loop(0, pairs, place_pair, 0)

    core = me[1]
    here = ring_place(me[0], worker_count)
    middle, half = worker_count // 2, image_count // 2
    narrow = table[LEVEL, 0] == 0
    for column in range(8):
        place = jnp.where(core == 0, FIRST[column], SECOND[column])
        wide_place = jnp.where(core == 0, column, (column + 4) % 8)
        place = jnp.where(narrow, place, wide_place)
        slot = place // 2
        used = slot < load[here]
        view = first[members[here * MOST + slot]] + lax.rem(place, 2)
        owner, row = owners[view], locals_[view]
        gap = lax.rem(ring_place(owner, worker_count) - here + worker_count, worker_count)
        late = jnp.logical_and(gap == middle, row >= half)
        part = jnp.where(late, worker_count, gap)
        table[0, column] = jnp.where(used, part, 0)
        table[1, column] = jnp.where(used, jnp.where(late, row - half, row), 0)
        table[2, column] = owner * image_count + row
        table[3, column] = core
        table[4, column] = jnp.where(used, 1, 0)


def plan(owners, locals_, counts, worker, core, image_count, worker_count):
    requests = locals_.shape[0] // worker_count
    share = requests // 4
    place = jnp.where(core == 0, jnp.array(FIRST, jnp.int32), jnp.array(SECOND, jnp.int32))
    pair = worker * share + place // 2
    workers = jnp.arange(worker_count, dtype=jnp.int32)
    upto = jnp.sum(
        jnp.where(workers[None, :] <= workers[:, None], counts[None, :], 0), axis=1
    )
    past = upto[None, :] <= pair[:, None]
    holder = jnp.sum(past.astype(jnp.int32), axis=1)
    slot = pair - jnp.sum(jnp.where(past, counts[None, :], 0), axis=1)
    view = holder * requests + slot * 2 + place % 2
    all_images = owners * image_count + locals_
    ids = jnp.arange(all_images.shape[0], dtype=jnp.int32)
    image = jnp.sum(jnp.where(view[:, None] == ids[None, :], all_images[None, :], 0), axis=1)
    owner, row = image // image_count, image % image_count
    gap = (ring_place(owner, worker_count) - ring_place(worker, worker_count)) % worker_count
    middle, half = worker_count // 2, image_count // 2
    late = jnp.logical_and(gap == middle, row >= half)
    part = jnp.where(late, worker_count, gap)
    row = jnp.where(late, row - half, row)
    head = jnp.broadcast_to(jnp.asarray(core, jnp.int32), (8,))
    return jnp.stack([part, row, image, head, jnp.ones_like(image)])


def fetch(table, column, keys, parts, target, sem, wait):
    if wait:
        pltpu.make_async_copy(parts[0].at[0], target, sem).wait()
        return
    part, row = table[0, column], table[1, column]
    for key, source in zip(keys, parts, strict=True):

        @pl.when(part == key)
        def _():
            pltpu.make_async_copy(source.at[row], target, sem).start()


def pick_kernel(keys, first_column, table, *refs):
    parts, (out, sems) = refs[: len(keys)], refs[-2:]
    for wait in (False, True):
        for j in range(4):
            fetch(table, first_column + j, keys, parts, out.at[j], sems.at[j], wait)


def pick(table, parts, first_column, held):
    keys = sorted(parts)
    hold = in_vmem if len(keys) < 10 else in_hbm
    space = pltpu.VMEM if len(keys) < 10 else pltpu.HBM
    _, rows, half = parts[0].shape
    return pl.pallas_call(
        functools.partial(pick_kernel, keys, first_column),
        out_shape=jax.ShapeDtypeStruct((4, rows, half), BF16),
        in_specs=[pl.BlockSpec(memory_space=pltpu.SMEM)]
        + [pl.BlockSpec(memory_space=space)] * len(keys)
        + [pl.BlockSpec(memory_space=pltpu.VMEM)] * len(held),
        out_specs=pl.BlockSpec(memory_space=pltpu.VMEM),
        scratch_shapes=[pltpu.SemaphoreType.DMA((4,))],
        compiler_params=pltpu.CompilerParams(vmem_limit_bytes=8 * 1024 * 1024),
        cost_estimate=pl.CostEstimate(
            flops=0, bytes_accessed=16 * rows * half, transcendentals=0
        ),
        name="pick",
    )(table, *[hold(parts[key]) for key in keys], *[in_vmem(array) for array in held])


def stage_kernel(count, *refs):
    sources, targets, sems = refs[:count], refs[count : 2 * count], refs[2 * count]
    copies = [pltpu.make_async_copy(sources[i], targets[i], sems.at[i]) for i in range(count)]
    for copy in copies:
        copy.start()
    for copy in copies:
        copy.wait()


def stage(arrays):
    count = len(arrays)
    size = sum(array.size * array.dtype.itemsize for array in arrays)
    return pl.pallas_call(
        functools.partial(stage_kernel, count),
        out_shape=tuple(jax.ShapeDtypeStruct(array.shape, array.dtype) for array in arrays),
        in_specs=[pl.BlockSpec(memory_space=pltpu.HBM)] * count,
        out_specs=(pl.BlockSpec(memory_space=pltpu.VMEM),) * count,
        scratch_shapes=[pltpu.SemaphoreType.DMA((count,))],
        compiler_params=pltpu.CompilerParams(vmem_limit_bytes=16 * 1024 * 1024),
        cost_estimate=pl.CostEstimate(flops=0, bytes_accessed=2 * size, transcendentals=0),
        name="stage",
    )(*[in_hbm(array) for array in arrays])


def gather_images(table, parts, held):
    other = lax.ppermute(pick(table, parts, 4, held), "mp", [(0, 1), (1, 0)])
    return pick(table, parts, 0, held), other


def norm_last(rows, gain):
    average = jnp.mean(rows, axis=-1, keepdims=True)
    centered = rows - average
    variance = jnp.mean(centered * centered, axis=-1, keepdims=True)
    return centered * lax.rsqrt(variance + EPS) * gain


def decode_kernel(tokens, table, *refs):
    (mine, theirs, gain_q, gain_c, gain_h, bias_h, wp) = refs[:7]
    wq, wk, wv, wo, wh = refs[7:12]
    out = refs[12]
    (xq, xc, res, q, k, v, att, hid) = refs[13:]
    rows, half = mine.shape[1], mine.shape[2]
    views, padded, width = q.shape
    core = table[3, 0]

    out[...] = jnp.zeros_like(out)
    tail = jnp.zeros((views, padded - rows, width), BF16)
    xq[:, rows:, :] = tail
    xc[:, rows:, :] = tail
    res[:, rows:, :] = tail

    here = pl.ds(pl.multiple_of(core * half, half), half)
    there = pl.ds(pl.multiple_of((1 - core) * half, half), half)
    context_of = (1, 0, None, 2) if views == 3 else (1, 0, 3, 2)
    for j in range(4):
        raw_a, raw_b = mine[j], theirs[j]
        a, b = raw_a.astype(F32), raw_b.astype(F32)
        average = (
            jnp.sum(a, axis=-1, keepdims=True) + jnp.sum(b, axis=-1, keepdims=True)
        ) / width
        a, b = a - average, b - average
        variance = (
            jnp.sum(a * a, axis=-1, keepdims=True) + jnp.sum(b * b, axis=-1, keepdims=True)
        ) / width
        scale = lax.rsqrt(variance + EPS)
        a, b = a * scale, b * scale
        if j < views:
            xq[j, :rows, here] = (a * gain_q[:, here]).astype(BF16)
            xq[j, :rows, there] = (b * gain_q[:, there]).astype(BF16)
            res[j, :rows, here] = raw_a
            res[j, :rows, there] = raw_b
        if context_of[j] is not None:
            xc[context_of[j], :rows, here] = (a * gain_c[:, here]).astype(BF16)
            xc[context_of[j], :rows, there] = (b * gain_c[:, there]).astype(BF16)

    total = views * padded
    head_size = width // HEADS
    queries = xq[...].reshape(total, width)
    contexts = xc[...].reshape(total, width)
    proj = jnp.dot(queries, wq[...], preferred_element_type=F32)
    q[...] = (proj.astype(BF16) * BF16(head_size**-0.5)).reshape(views, padded, width)
    proj = jnp.dot(contexts, wk[...], preferred_element_type=F32)
    k[...] = proj.astype(BF16).reshape(views, padded, width)
    proj = jnp.dot(contexts, wv[...], preferred_element_type=F32)
    v[...] = proj.astype(BF16).reshape(views, padded, width)

    block = 2 * head_size
    low = lax.broadcasted_iota(jnp.int32, (padded, block), 1) < head_size
    hide = jnp.where(lax.broadcasted_iota(jnp.int32, (1, padded), 1) < tokens, 0.0, -1e30)
    nothing = jnp.zeros((padded, block), BF16)

    def attend(i, carry):
        for b in range(width // block):
            cols = slice(b * block, (b + 1) * block)
            qb, kb, vb = q[i, :, cols], k[i, :, cols], v[i, :, cols]
            blended = []
            for keep in (0, 1):
                qh = jnp.where(low, qb, nothing) if keep == 0 else jnp.where(low, nothing, qb)
                scores = lax.dot_general(
                    qh, kb, (((1,), (1,)), ((), ())), preferred_element_type=F32
                )
                scores = scores + hide
                peak = jnp.max(scores, axis=-1, keepdims=True)
                expo = jnp.exp(scores - peak)
                inverse = 1.0 / jnp.sum(expo, axis=-1, keepdims=True)
                probs = (expo * inverse).astype(BF16)
                blended.append(jnp.dot(probs, vb, preferred_element_type=F32))
            att[i, :, cols] = jnp.where(low, blended[0], blended[1]).astype(BF16)
        return carry

    lax.fori_loop(0, views, attend, 0)

    updated = jnp.dot(att[...].reshape(total, width), wo[...], preferred_element_type=F32)
    updated = updated + res[...].reshape(total, width).astype(F32)
    head_in = norm_last(updated, gain_h[...]).astype(BF16)
    hidden = jnp.dot(head_in, wh[...], preferred_element_type=F32) + bias_h[...]
    hid[...] = jax.nn.gelu(hidden).astype(BF16).reshape(views, padded, hid.shape[2])
    for i in range(views):
        raw = lax.dot_general(
            wp[...], hid[i], (((1,), (1,)), ((), ())), preferred_element_type=F32
        )
        conf = 1.0 + jnp.exp(raw[3:4])
        last = lax.broadcasted_iota(jnp.int32, raw.shape, 0) == 3
        contrib = jnp.where(last, conf, raw * conf)
        image = table[2, i]

        @pl.when(table[4, i] == 1)
        def _():
            out[image] = out[image] + contrib[:, :tokens]


def per_device(
    tokens,
    gain_query,
    gain_context,
    query_weight,
    key_weight,
    value_weight,
    out_weight,
    gain_head,
    hidden_weight,
    hidden_bias,
    point_weight,
    view_owner,
    view_local,
    pair_count,
):
    worker_count = lax.axis_size("pairs")
    core_count = lax.axis_size("mp")
    worker = lax.axis_index("pairs").astype(jnp.int32)
    core = lax.axis_index("mp").astype(jnp.int32)
    image_count, token_count, half = tokens.shape
    width, hidden_width = hidden_weight.shape
    rows = -(-token_count // 8) * 8
    padded = -(-token_count // 16) * 16

    shard = jnp.pad(tokens, ((0, 0), (0, rows - token_count), (0, 0)))
    scalars = pl.BlockSpec(memory_space=pltpu.SMEM)
    vector = pl.BlockSpec(memory_space=pltpu.VMEM)
    owners = view_owner[:, 0]
    weights = stage((query_weight, key_weight, value_weight, out_weight, hidden_weight))
    vectors = (
        gain_query.reshape(1, width),
        gain_context.reshape(1, width),
        gain_head.reshape(1, width),
        hidden_bias.reshape(1, hidden_width),
        point_weight,
    )

    def decode(views, table, parts, vectors, weights):
        wide = pltpu.VMEM((views, padded, width), BF16)
        keep, other = gather_images(table, parts, weights)
        return pl.pallas_call(
            functools.partial(decode_kernel, token_count),
            out_shape=jax.ShapeDtypeStruct((worker_count * image_count, 4, token_count), F32),
            in_specs=[scalars] + [vector] * 12,
            out_specs=vector,
            scratch_shapes=[wide] * 7 + [pltpu.VMEM((views, padded, hidden_width), BF16)],
            compiler_params=pltpu.CompilerParams(vmem_limit_bytes=32 * 1024 * 1024),
            name="decode",
        )(table, in_vmem(keep), in_vmem(other), *vectors, *[in_vmem(w) for w in weights])

    if worker_count == 8:
        reach = 2
        pairs = worker_count * SHARE
        table = pl.pallas_call(
            functools.partial(deal_kernel, worker_count, image_count, reach),
            out_shape=jax.ShapeDtypeStruct((LEVEL + 1, 8), jnp.int32),
            in_specs=[scalars] * 4,
            out_specs=scalars,
            scratch_shapes=[pltpu.SMEM((pairs,), jnp.int32)] * 4
            + [pltpu.SMEM((worker_count,), jnp.int32)]
            + [pltpu.SMEM((worker_count * MOST,), jnp.int32)]
            + [pltpu.SMEM((worker_count,), jnp.int32)],
            compiler_params=pltpu.CompilerParams(vmem_limit_bytes=2 * 1024 * 1024),
            cost_estimate=pl.CostEstimate(flops=0, bytes_accessed=20 * 10**6, transcendentals=0),
            name="deal",
        )(owners, view_local, pair_count, jnp.stack([worker, core]))
        parts = ring_near(shard, worker_count, reach)

        def decode_far(table, near, *rest):
            return decode(MOST, table, ring_far(near, worker_count, reach), *rest)

        flat = lax.switch(
            table[LEVEL, 0],
            (functools.partial(decode, SHARE), functools.partial(decode, MOST), decode_far),
            table,
            parts,
            vectors,
            weights,
        )
    else:
        table = plan(owners, view_local, pair_count, worker, core, image_count, worker_count)
        parts = ring_far({0: shard, worker_count: shard}, worker_count, 0)
        flat = decode(SHARE, table, parts, vectors, weights)
    arrived = lax.all_to_all(flat, ("pairs", "mp"), 0, 0, tiled=True)
    mine = image_count // core_count
    return jnp.sum(arrived.reshape(worker_count * core_count, mine, 4, token_count), axis=0)


def solution(mesh):
    return jax.shard_map(
        per_device,
        mesh=mesh,
        in_specs=(
            P(("groups", "pairs"), None, "mp"),
            P(),
            P(),
            P(),
            P(),
            P(),
            P(),
            P(),
            P(),
            P(),
            P(),
            P("groups", None),
            P("groups"),
            P("groups"),
        ),
        out_specs=P(("groups", "pairs", "mp"), None, None),
        check_vma=False,
    )
```

```python
import functools

import jax
import jax.numpy as jnp
from jax import lax
from jax.experimental import pallas as pl
from jax.experimental.pallas import tpu as pltpu
from jax.sharding import PartitionSpec as P

HEADS = 12
EPS = 1e-06
F32 = jnp.float32
BF16 = jnp.bfloat16


def in_hbm(array):
    return pltpu.with_memory_space_constraint(array, pltpu.HBM)


def in_vmem(array):
    return pltpu.with_memory_space_constraint(array, pltpu.VMEM)


def ring_place(index, count):
    if count > 8:
        return index
    half = index // 2
    return jnp.where(index % 2 == 0, half, count - 1 - half)


def ring_order(count):
    if count > 8:
        return list(range(count))
    return list(range(0, count, 2)) + list(range(count - 1, 0, -2))


def ring_steps(worker_count):
    order = ring_order(worker_count)
    ahead = [(order[i], order[(i + 1) % worker_count]) for i in range(worker_count)]
    return ahead, [(b, a) for a, b in ahead]


def ring_near(shard, worker_count, reach):
    ahead, back = ring_steps(worker_count)
    parts = {0: shard}
    going, coming = shard, shard
    for step in range(1, reach + 1):
        going = lax.ppermute(going, "pairs", ahead)
        coming = lax.ppermute(coming, "pairs", back)
        parts[worker_count - step] = going
        parts[step] = coming
    return parts


def ring_far(parts, worker_count, reach):
    ahead, back = ring_steps(worker_count)
    middle = worker_count // 2
    parts = dict(parts)
    going, coming = parts[worker_count - reach], parts[reach]
    half = going.shape[0] // 2
    for step in range(reach + 1, middle):
        going = lax.ppermute(going, "pairs", ahead)
        coming = lax.ppermute(coming, "pairs", back)
        parts[worker_count - step] = going
        parts[step] = coming
    parts[middle] = lax.ppermute(going[:half], "pairs", ahead)
    parts[worker_count] = lax.ppermute(coming[half:], "pairs", back)
    return parts


FIRST = (0, 1, 2, 3, 4, 5, 3, 2)
SECOND = (4, 5, 3, 2, 0, 1, 2, 3)
SHARE = 3
MOST = 4
LEVEL = 5


def deal_kernel(
    worker_count,
    image_count,
    reach,
    owners,
    locals_,
    counts,
    me,
    table,
    first,
    fits,
    holder,
    spot,
    load,
    members,
    parent,
):
    requests = owners.shape[0] // worker_count
    pairs = worker_count * SHARE
    everyone = 2**worker_count - 1

    def list_worker(w, r):
        def list_slot(s, r):
            first[r] = w * requests + 2 * s
            return r + 1

        return lax.fori_loop(0, counts[w], list_slot, r)

    lax.fori_loop(0, worker_count, list_worker, 0)

    def near(view):
        place = ring_place(owners[view], worker_count)
        turned = (2 ** (2 * reach + 1) - 1) << lax.rem(place + worker_count - reach, worker_count)
        return (turned | (turned >> worker_count)) & everyone

    def set_pair(r, carry):
        fits[r] = near(first[r]) & near(first[r] + 1)
        holder[r] = -1
        spot[r] = 0
        return carry

    lax.fori_loop(0, pairs, set_pair, 0)
    for w in range(worker_count):
        load[w] = 0
        for x in range(MOST):
            members[w * MOST + x] = 0

    def put(pair, w, slot):
        members[w * MOST + slot] = pair
        holder[pair] = w
        spot[pair] = slot

    def match(most, r):
        for w in range(worker_count):
            parent[w] = r

        def searching(state):
            seen, done, found = state
            return jnp.logical_and(found < 0, (seen & ~done) != 0)

        def search(state):
            seen, done, found = state
            todo = seen & ~done
            w = jnp.int32(0)
            for x in range(worker_count - 1, -1, -1):
                w = jnp.where(((todo >> x) & 1) == 1, jnp.int32(x), w)
            room = load[w] < most
            fresh_all = jnp.int32(0)
            for i in range(most):
                q = jnp.where(room, r, members[w * MOST + i])
                fresh = jnp.where(room, 0, fits[q] & ~(seen | fresh_all))
                for x in range(worker_count):

                    @pl.when(((fresh >> x) & 1) == 1)
                    def _():
                        parent[x] = q

                fresh_all = fresh_all | fresh
            return seen | fresh_all, done | (1 << w), jnp.where(room, w, found)

        start = (fits[r], jnp.int32(0), jnp.int32(-1))
        _, _, found = lax.while_loop(searching, search, start)

        @pl.when(found >= 0)
        def _():
            def moving(state):
                return state[0] >= 0

            def move(state):
                w, slot = state
                pair = parent[w]
                after = (holder[pair], spot[pair])
                put(pair, w, slot)
                return after

            slot = load[found]
            load[found] = slot + 1
            lax.while_loop(moving, move, (found, slot))

        return jnp.where(found < 0, 1, 0)

    missed = lax.fori_loop(0, pairs, lambda r, m: m + match(SHARE, r), jnp.int32(0))
    table[LEVEL, 0] = jnp.where(missed > 0, 1, 0)

    @pl.when(missed > 0)
    def _():
        def again(r, left):
            lost = jnp.where(holder[r] < 0, 1, 0)

            @pl.when(lost == 1)
            def _():
                match(MOST, r)

            return left + jnp.where(holder[r] < 0, 1, 0)

        left = lax.fori_loop(0, pairs, again, jnp.int32(0))

        @pl.when(left > 0)
        def _():
            table[LEVEL, 0] = 2

            def place_pair(r, carry):
                def try_worker(w, carry):
                    @pl.when(jnp.logical_and(holder[r] < 0, load[w] < MOST))
                    def _():
                        put(r, w, load[w])
                        load[w] = load[w] + 1

                    return carry

                return lax.fori_loop(0, worker_count, try_worker, carry)

            lax.fori_loop(0, pairs, place_pair, 0)

    core = me[1]
    here = ring_place(me[0], worker_count)
    middle, half = worker_count // 2, image_count // 2
    narrow = table[LEVEL, 0] == 0
    for column in range(8):
        place = jnp.where(core == 0, FIRST[column], SECOND[column])
        wide_place = jnp.where(core == 0, column, (column + 4) % 8)
        place = jnp.where(narrow, place, wide_place)
        slot = place // 2
        used = slot < load[here]
        view = first[members[here * MOST + slot]] + lax.rem(place, 2)
        owner, row = owners[view], locals_[view]
        gap = lax.rem(ring_place(owner, worker_count) - here + worker_count, worker_count)
        late = jnp.logical_and(gap == middle, row >= half)
        part = jnp.where(late, worker_count, gap)
        table[0, column] = jnp.where(used, part, 0)
        table[1, column] = jnp.where(used, jnp.where(late, row - half, row), 0)
        table[2, column] = owner * image_count + row
        table[3, column] = core
        table[4, column] = jnp.where(used, 1, 0)


def plan(owners, locals_, counts, worker, core, image_count, worker_count):
    requests = locals_.shape[0] // worker_count
    share = requests // 4
    place = jnp.where(core == 0, jnp.array(FIRST, jnp.int32), jnp.array(SECOND, jnp.int32))
    pair = worker * share + place // 2
    workers = jnp.arange(worker_count, dtype=jnp.int32)
    upto = jnp.sum(
        jnp.where(workers[None, :] <= workers[:, None], counts[None, :], 0), axis=1
    )
    past = upto[None, :] <= pair[:, None]
    holder = jnp.sum(past.astype(jnp.int32), axis=1)
    slot = pair - jnp.sum(jnp.where(past, counts[None, :], 0), axis=1)
    view = holder * requests + slot * 2 + place % 2
    all_images = owners * image_count + locals_
    ids = jnp.arange(all_images.shape[0], dtype=jnp.int32)
    image = jnp.sum(jnp.where(view[:, None] == ids[None, :], all_images[None, :], 0), axis=1)
    owner, row = image // image_count, image % image_count
    gap = (ring_place(owner, worker_count) - ring_place(worker, worker_count)) % worker_count
    middle, half = worker_count // 2, image_count // 2
    late = jnp.logical_and(gap == middle, row >= half)
    part = jnp.where(late, worker_count, gap)
    row = jnp.where(late, row - half, row)
    head = jnp.broadcast_to(jnp.asarray(core, jnp.int32), (8,))
    return jnp.stack([part, row, image, head, jnp.ones_like(image)])


def fetch(table, column, keys, parts, target, sem, wait):
    if wait:
        pltpu.make_async_copy(parts[0].at[0], target, sem).wait()
        return
    part, row = table[0, column], table[1, column]
    for key, source in zip(keys, parts, strict=True):

        @pl.when(part == key)
        def _():
            pltpu.make_async_copy(source.at[row], target, sem).start()


def pick_kernel(keys, first_column, table, *refs):
    parts, (out, sems) = refs[: len(keys)], refs[-2:]
    for wait in (False, True):
        for j in range(4):
            fetch(table, first_column + j, keys, parts, out.at[j], sems.at[j], wait)


def pick(table, parts, first_column, held):
    keys = sorted(parts)
    hold = in_vmem if len(keys) < 10 else in_hbm
    space = pltpu.VMEM if len(keys) < 10 else pltpu.HBM
    _, rows, half = parts[0].shape
    return pl.pallas_call(
        functools.partial(pick_kernel, keys, first_column),
        out_shape=jax.ShapeDtypeStruct((4, rows, half), BF16),
        in_specs=[pl.BlockSpec(memory_space=pltpu.SMEM)]
        + [pl.BlockSpec(memory_space=space)] * len(keys)
        + [pl.BlockSpec(memory_space=pltpu.VMEM)] * len(held),
        out_specs=pl.BlockSpec(memory_space=pltpu.VMEM),
        scratch_shapes=[pltpu.SemaphoreType.DMA((4,))],
        compiler_params=pltpu.CompilerParams(vmem_limit_bytes=8 * 1024 * 1024),
        cost_estimate=pl.CostEstimate(
            flops=0, bytes_accessed=16 * rows * half, transcendentals=0
        ),
        name="pick",
    )(table, *[hold(parts[key]) for key in keys], *[in_vmem(array) for array in held])


def stage_kernel(count, *refs):
    sources, targets, sems = refs[:count], refs[count : 2 * count], refs[2 * count]
    copies = [pltpu.make_async_copy(sources[i], targets[i], sems.at[i]) for i in range(count)]
    for copy in copies:
        copy.start()
    for copy in copies:
        copy.wait()


def stage(arrays):
    count = len(arrays)
    size = sum(array.size * array.dtype.itemsize for array in arrays)
    return pl.pallas_call(
        functools.partial(stage_kernel, count),
        out_shape=tuple(jax.ShapeDtypeStruct(array.shape, array.dtype) for array in arrays),
        in_specs=[pl.BlockSpec(memory_space=pltpu.HBM)] * count,
        out_specs=(pl.BlockSpec(memory_space=pltpu.VMEM),) * count,
        scratch_shapes=[pltpu.SemaphoreType.DMA((count,))],
        compiler_params=pltpu.CompilerParams(vmem_limit_bytes=16 * 1024 * 1024),
        cost_estimate=pl.CostEstimate(flops=0, bytes_accessed=2 * size, transcendentals=0),
        name="stage",
    )(*[in_hbm(array) for array in arrays])


def gather_images(table, parts, held):
    other = lax.ppermute(pick(table, parts, 4, held), "mp", [(0, 1), (1, 0)])
    return pick(table, parts, 0, held), other


def norm_last(rows, gain):
    average = jnp.mean(rows, axis=-1, keepdims=True)
    centered = rows - average
    variance = jnp.mean(centered * centered, axis=-1, keepdims=True)
    return centered * lax.rsqrt(variance + EPS) * gain


def decode_kernel(tokens, table, *refs):
    (mine, theirs, gain_q, gain_c, gain_h, bias_h, wp) = refs[:7]
    wq, wk, wv, wo, wh = refs[7:12]
    out = refs[12]
    (xq, xc, res, q, k, v, att, hid) = refs[13:]
    rows, half = mine.shape[1], mine.shape[2]
    views, padded, width = q.shape
    core = table[3, 0]

    out[...] = jnp.zeros_like(out)
    tail = jnp.zeros((views, padded - rows, width), BF16)
    xq[:, rows:, :] = tail
    xc[:, rows:, :] = tail
    res[:, rows:, :] = tail

    here = pl.ds(pl.multiple_of(core * half, half), half)
    there = pl.ds(pl.multiple_of((1 - core) * half, half), half)
    context_of = (1, 0, None, 2) if views == 3 else (1, 0, 3, 2)
    for j in range(4):
        raw_a, raw_b = mine[j], theirs[j]
        a, b = raw_a.astype(F32), raw_b.astype(F32)
        average = (
            jnp.sum(a, axis=-1, keepdims=True) + jnp.sum(b, axis=-1, keepdims=True)
        ) / width
        a, b = a - average, b - average
        variance = (
            jnp.sum(a * a, axis=-1, keepdims=True) + jnp.sum(b * b, axis=-1, keepdims=True)
        ) / width
        scale = lax.rsqrt(variance + EPS)
        a, b = a * scale, b * scale
        if j < views:
            xq[j, :rows, here] = (a * gain_q[:, here]).astype(BF16)
            xq[j, :rows, there] = (b * gain_q[:, there]).astype(BF16)
            res[j, :rows, here] = raw_a
            res[j, :rows, there] = raw_b
        if context_of[j] is not None:
            xc[context_of[j], :rows, here] = (a * gain_c[:, here]).astype(BF16)
            xc[context_of[j], :rows, there] = (b * gain_c[:, there]).astype(BF16)

    total = views * padded
    head_size = width // HEADS
    queries = xq[...].reshape(total, width)
    contexts = xc[...].reshape(total, width)
    proj = jnp.dot(queries, wq[...], preferred_element_type=F32)
    q[...] = (proj.astype(BF16) * BF16(head_size**-0.5)).reshape(views, padded, width)
    proj = jnp.dot(contexts, wk[...], preferred_element_type=F32)
    k[...] = proj.astype(BF16).reshape(views, padded, width)
    proj = jnp.dot(contexts, wv[...], preferred_element_type=F32)
    v[...] = proj.astype(BF16).reshape(views, padded, width)

    block = 2 * head_size
    low = lax.broadcasted_iota(jnp.int32, (padded, block), 1) < head_size
    hide = jnp.where(lax.broadcasted_iota(jnp.int32, (1, padded), 1) < tokens, 0.0, -1e30)
    nothing = jnp.zeros((padded, block), BF16)

    def attend(i, carry):
        for b in range(width // block):
            cols = slice(b * block, (b + 1) * block)
            qb, kb, vb = q[i, :, cols], k[i, :, cols], v[i, :, cols]
            qh = jnp.concatenate([jnp.where(low, qb, nothing), jnp.where(low, nothing, qb)], axis=0)
            scores = lax.dot_general(
                qh, kb, (((1,), (1,)), ((), ())), preferred_element_type=F32
            )
            scores = scores + hide
            peak = jnp.max(scores, axis=-1, keepdims=True)
            expo = jnp.exp(scores - peak)
            inverse = 1.0 / jnp.sum(expo, axis=-1, keepdims=True)
            probs = (expo * inverse).astype(BF16)
            both = jnp.dot(probs, vb, preferred_element_type=F32)
            blended = (both[:padded], both[padded:])
            att[i, :, cols] = jnp.where(low, blended[0], blended[1]).astype(BF16)
        return carry

    if views == SHARE:
        for i in range(views):
            attend(i, 0)
    else:
        lax.fori_loop(0, views, attend, 0)

    updated = jnp.dot(att[...].reshape(total, width), wo[...], preferred_element_type=F32)
    updated = updated + res[...].reshape(total, width).astype(F32)
    head_in = norm_last(updated, gain_h[...]).astype(BF16)
    hidden = jnp.dot(head_in, wh[...], preferred_element_type=F32) + bias_h[...]
    hid[...] = jax.nn.gelu(hidden).astype(BF16).reshape(views, padded, hid.shape[2])
    for i in range(views):
        raw = lax.dot_general(
            wp[...], hid[i], (((1,), (1,)), ((), ())), preferred_element_type=F32
        )
        conf = 1.0 + jnp.exp(raw[3:4])
        last = lax.broadcasted_iota(jnp.int32, raw.shape, 0) == 3
        contrib = jnp.where(last, conf, raw * conf)
        image = table[2, i]

        @pl.when(table[4, i] == 1)
        def _():
            out[image] = out[image] + contrib[:, :tokens]


def per_device(
    tokens,
    gain_query,
    gain_context,
    query_weight,
    key_weight,
    value_weight,
    out_weight,
    gain_head,
    hidden_weight,
    hidden_bias,
    point_weight,
    view_owner,
    view_local,
    pair_count,
):
    worker_count = lax.axis_size("pairs")
    core_count = lax.axis_size("mp")
    worker = lax.axis_index("pairs").astype(jnp.int32)
    core = lax.axis_index("mp").astype(jnp.int32)
    image_count, token_count, half = tokens.shape
    width, hidden_width = hidden_weight.shape
    rows = -(-token_count // 8) * 8
    padded = -(-token_count // 16) * 16

    shard = jnp.pad(tokens, ((0, 0), (0, rows - token_count), (0, 0)))
    scalars = pl.BlockSpec(memory_space=pltpu.SMEM)
    vector = pl.BlockSpec(memory_space=pltpu.VMEM)
    owners = view_owner[:, 0]
    weights = stage((query_weight, key_weight, value_weight, out_weight, hidden_weight))
    vectors = (
        gain_query.reshape(1, width),
        gain_context.reshape(1, width),
        gain_head.reshape(1, width),
        hidden_bias.reshape(1, hidden_width),
        point_weight,
    )

    def decode(views, table, parts, vectors, weights):
        wide = pltpu.VMEM((views, padded, width), BF16)
        keep, other = gather_images(table, parts, weights)
        return pl.pallas_call(
            functools.partial(decode_kernel, token_count),
            out_shape=jax.ShapeDtypeStruct((worker_count * image_count, 4, token_count), F32),
            in_specs=[scalars] + [vector] * 12,
            out_specs=vector,
            scratch_shapes=[wide] * 7 + [pltpu.VMEM((views, padded, hidden_width), BF16)],
            compiler_params=pltpu.CompilerParams(vmem_limit_bytes=32 * 1024 * 1024),
            name="decode",
        )(table, in_vmem(keep), in_vmem(other), *vectors, *[in_vmem(w) for w in weights])

    if worker_count == 8:
        reach = 2
        pairs = worker_count * SHARE
        table = pl.pallas_call(
            functools.partial(deal_kernel, worker_count, image_count, reach),
            out_shape=jax.ShapeDtypeStruct((LEVEL + 1, 8), jnp.int32),
            in_specs=[scalars] * 4,
            out_specs=scalars,
            scratch_shapes=[pltpu.SMEM((pairs,), jnp.int32)] * 4
            + [pltpu.SMEM((worker_count,), jnp.int32)]
            + [pltpu.SMEM((worker_count * MOST,), jnp.int32)]
            + [pltpu.SMEM((worker_count,), jnp.int32)],
            compiler_params=pltpu.CompilerParams(vmem_limit_bytes=2 * 1024 * 1024),
            cost_estimate=pl.CostEstimate(flops=0, bytes_accessed=20 * 10**6, transcendentals=0),
            name="deal",
        )(owners, view_local, pair_count, jnp.stack([worker, core]))
        parts = ring_near(shard, worker_count, reach)

        def decode_far(table, near, *rest):
            return decode(MOST, table, ring_far(near, worker_count, reach), *rest)

        flat = lax.switch(
            table[LEVEL, 0],
            (functools.partial(decode, SHARE), functools.partial(decode, MOST), decode_far),
            table,
            parts,
            vectors,
            weights,
        )
    else:
        table = plan(owners, view_local, pair_count, worker, core, image_count, worker_count)
        parts = ring_far({0: shard, worker_count: shard}, worker_count, 0)
        flat = decode(SHARE, table, parts, vectors, weights)
    arrived = lax.all_to_all(flat, ("pairs", "mp"), 0, 0, tiled=True)
    mine = image_count // core_count
    return jnp.sum(arrived.reshape(worker_count * core_count, mine, 4, token_count), axis=0)


def solution(mesh):
    return jax.shard_map(
        per_device,
        mesh=mesh,
        in_specs=(
            P(("groups", "pairs"), None, "mp"),
            P(),
            P(),
            P(),
            P(),
            P(),
            P(),
            P(),
            P(),
            P(),
            P(),
            P("groups", None),
            P("groups"),
            P("groups"),
        ),
        out_specs=P(("groups", "pairs", "mp"), None, None),
        check_vma=False,
    )
```

```python
import functools

import jax
import jax.numpy as jnp
from jax import lax
from jax.experimental import pallas as pl
from jax.experimental.pallas import tpu as pltpu
from jax.sharding import PartitionSpec as P

HEADS = 12
EPS = 1e-06
F32 = jnp.float32
BF16 = jnp.bfloat16


def in_hbm(array):
    return pltpu.with_memory_space_constraint(array, pltpu.HBM)


def in_vmem(array):
    return pltpu.with_memory_space_constraint(array, pltpu.VMEM)


def ring_place(index, count):
    if count > 8:
        return index
    half = index // 2
    return jnp.where(index % 2 == 0, half, count - 1 - half)


def ring_order(count):
    if count > 8:
        return list(range(count))
    return list(range(0, count, 2)) + list(range(count - 1, 0, -2))


def ring_steps(worker_count):
    order = ring_order(worker_count)
    ahead = [(order[i], order[(i + 1) % worker_count]) for i in range(worker_count)]
    return ahead, [(b, a) for a, b in ahead]


def ring_near(shard, worker_count, reach):
    ahead, back = ring_steps(worker_count)
    parts = {0: shard}
    going, coming = shard, shard
    for step in range(1, reach + 1):
        going = lax.ppermute(going, "pairs", ahead)
        coming = lax.ppermute(coming, "pairs", back)
        parts[worker_count - step] = going
        parts[step] = coming
    return parts


def ring_far(parts, worker_count, reach):
    ahead, back = ring_steps(worker_count)
    middle = worker_count // 2
    parts = dict(parts)
    going, coming = parts[worker_count - reach], parts[reach]
    half = going.shape[0] // 2
    for step in range(reach + 1, middle):
        going = lax.ppermute(going, "pairs", ahead)
        coming = lax.ppermute(coming, "pairs", back)
        parts[worker_count - step] = going
        parts[step] = coming
    parts[middle] = lax.ppermute(going[:half], "pairs", ahead)
    parts[worker_count] = lax.ppermute(coming[half:], "pairs", back)
    return parts


FIRST = (0, 1, 2, 3, 4, 5, 3, 2)
SECOND = (4, 5, 3, 2, 0, 1, 2, 3)
SHARE = 3
MOST = 4
LEVEL = 5
SPOT = 6


def deal_kernel(
    worker_count,
    image_count,
    reach,
    owners,
    locals_,
    counts,
    me,
    table,
    first,
    fits,
    holder,
    spot,
    load,
    members,
    parent,
):
    requests = owners.shape[0] // worker_count
    pairs = worker_count * SHARE
    everyone = 2**worker_count - 1

    def list_worker(w, r):
        def list_slot(s, r):
            first[r] = w * requests + 2 * s
            return r + 1

        return lax.fori_loop(0, counts[w], list_slot, r)

    lax.fori_loop(0, worker_count, list_worker, 0)

    def near(view):
        place = ring_place(owners[view], worker_count)
        turned = (2 ** (2 * reach + 1) - 1) << lax.rem(place + worker_count - reach, worker_count)
        return (turned | (turned >> worker_count)) & everyone

    def set_pair(r, carry):
        fits[r] = near(first[r]) & near(first[r] + 1)
        holder[r] = -1
        spot[r] = 0
        return carry

    lax.fori_loop(0, pairs, set_pair, 0)
    for w in range(worker_count):
        load[w] = 0
        for x in range(MOST):
            members[w * MOST + x] = 0

    def put(pair, w, slot):
        members[w * MOST + slot] = pair
        holder[pair] = w
        spot[pair] = slot

    def match(most, r):
        for w in range(worker_count):
            parent[w] = r

        def searching(state):
            seen, done, found = state
            return jnp.logical_and(found < 0, (seen & ~done) != 0)

        def search(state):
            seen, done, found = state
            todo = seen & ~done
            w = jnp.int32(0)
            for x in range(worker_count - 1, -1, -1):
                w = jnp.where(((todo >> x) & 1) == 1, jnp.int32(x), w)
            room = load[w] < most
            fresh_all = jnp.int32(0)
            for i in range(most):
                q = jnp.where(room, r, members[w * MOST + i])
                fresh = jnp.where(room, 0, fits[q] & ~(seen | fresh_all))
                for x in range(worker_count):

                    @pl.when(((fresh >> x) & 1) == 1)
                    def _():
                        parent[x] = q

                fresh_all = fresh_all | fresh
            return seen | fresh_all, done | (1 << w), jnp.where(room, w, found)

        start = (fits[r], jnp.int32(0), jnp.int32(-1))
        _, _, found = lax.while_loop(searching, search, start)

        @pl.when(found >= 0)
        def _():
            def moving(state):
                return state[0] >= 0

            def move(state):
                w, slot = state
                pair = parent[w]
                after = (holder[pair], spot[pair])
                put(pair, w, slot)
                return after

            slot = load[found]
            load[found] = slot + 1
            lax.while_loop(moving, move, (found, slot))

        return jnp.where(found < 0, 1, 0)

    missed = lax.fori_loop(0, pairs, lambda r, m: m + match(SHARE, r), jnp.int32(0))
    table[LEVEL, 0] = jnp.where(missed > 0, 1, 0)

    @pl.when(missed > 0)
    def _():
        def again(r, left):
            lost = jnp.where(holder[r] < 0, 1, 0)

            @pl.when(lost == 1)
            def _():
                match(MOST, r)

            return left + jnp.where(holder[r] < 0, 1, 0)

        left = lax.fori_loop(0, pairs, again, jnp.int32(0))

        @pl.when(left > 0)
        def _():
            table[LEVEL, 0] = 2

            def place_pair(r, carry):
                def try_worker(w, carry):
                    @pl.when(jnp.logical_and(holder[r] < 0, load[w] < MOST))
                    def _():
                        put(r, w, load[w])
                        load[w] = load[w] + 1

                    return carry

                return lax.fori_loop(0, worker_count, try_worker, carry)

            lax.fori_loop(0, pairs, place_pair, 0)

    core = me[1]
    here = ring_place(me[0], worker_count)
    middle, half = worker_count // 2, image_count // 2
    narrow = table[LEVEL, 0] == 0
    for column in range(8):
        place = jnp.where(core == 0, FIRST[column], SECOND[column])
        wide_place = jnp.where(core == 0, column, (column + 4) % 8)
        place = jnp.where(narrow, place, wide_place)
        slot = place // 2
        used = slot < load[here]
        view = first[members[here * MOST + slot]] + lax.rem(place, 2)
        owner, row = owners[view], locals_[view]
        gap = lax.rem(ring_place(owner, worker_count) - here + worker_count, worker_count)
        late = jnp.logical_and(gap == middle, row >= half)
        part = jnp.where(late, worker_count, gap)
        table[0, column] = jnp.where(used, part, 0)
        table[1, column] = jnp.where(used, jnp.where(late, row - half, row), 0)
        table[2, column] = owner * image_count + row
        table[3, column] = core
        table[4, column] = jnp.where(used, 1, 0)
        ahead = jnp.logical_or(gap == 1, gap == 2)
        nearest = jnp.logical_or(gap == 1, gap == worker_count - 1)
        ours = nearest == (core == 0)
        spot_there = jnp.where(ours, 0, 12) + jnp.where(ahead, 0, image_count) + row
        table[SPOT, column] = jnp.where(gap == 0, 2 * image_count + row, spot_there)


def plan(owners, locals_, counts, worker, core, image_count, worker_count):
    requests = locals_.shape[0] // worker_count
    share = requests // 4
    place = jnp.where(core == 0, jnp.array(FIRST, jnp.int32), jnp.array(SECOND, jnp.int32))
    pair = worker * share + place // 2
    workers = jnp.arange(worker_count, dtype=jnp.int32)
    upto = jnp.sum(
        jnp.where(workers[None, :] <= workers[:, None], counts[None, :], 0), axis=1
    )
    past = upto[None, :] <= pair[:, None]
    holder = jnp.sum(past.astype(jnp.int32), axis=1)
    slot = pair - jnp.sum(jnp.where(past, counts[None, :], 0), axis=1)
    view = holder * requests + slot * 2 + place % 2
    all_images = owners * image_count + locals_
    ids = jnp.arange(all_images.shape[0], dtype=jnp.int32)
    image = jnp.sum(jnp.where(view[:, None] == ids[None, :], all_images[None, :], 0), axis=1)
    owner, row = image // image_count, image % image_count
    gap = (ring_place(owner, worker_count) - ring_place(worker, worker_count)) % worker_count
    middle, half = worker_count // 2, image_count // 2
    late = jnp.logical_and(gap == middle, row >= half)
    part = jnp.where(late, worker_count, gap)
    row = jnp.where(late, row - half, row)
    head = jnp.broadcast_to(jnp.asarray(core, jnp.int32), (8,))
    return jnp.stack([part, row, image, head, jnp.ones_like(image)])


def fetch(table, column, keys, parts, target, sem, wait):
    if wait:
        pltpu.make_async_copy(parts[0].at[0], target, sem).wait()
        return
    part, row = table[0, column], table[1, column]
    for key, source in zip(keys, parts, strict=True):

        @pl.when(part == key)
        def _():
            pltpu.make_async_copy(source.at[row], target, sem).start()


def pick_kernel(keys, first_column, table, *refs):
    parts, (out, sems) = refs[: len(keys)], refs[-2:]
    for wait in (False, True):
        for j in range(4):
            fetch(table, first_column + j, keys, parts, out.at[j], sems.at[j], wait)


def pick(table, parts, first_column, held):
    keys = sorted(parts)
    hold = in_vmem if len(keys) < 10 else in_hbm
    space = pltpu.VMEM if len(keys) < 10 else pltpu.HBM
    _, rows, half = parts[0].shape
    return pl.pallas_call(
        functools.partial(pick_kernel, keys, first_column),
        out_shape=jax.ShapeDtypeStruct((4, rows, half), BF16),
        in_specs=[pl.BlockSpec(memory_space=pltpu.SMEM)]
        + [pl.BlockSpec(memory_space=space)] * len(keys)
        + [pl.BlockSpec(memory_space=pltpu.VMEM)] * len(held),
        out_specs=pl.BlockSpec(memory_space=pltpu.VMEM),
        scratch_shapes=[pltpu.SemaphoreType.DMA((4,))],
        compiler_params=pltpu.CompilerParams(vmem_limit_bytes=8 * 1024 * 1024),
        cost_estimate=pl.CostEstimate(
            flops=0, bytes_accessed=16 * rows * half, transcendentals=0
        ),
        name="pick",
    )(table, *[hold(parts[key]) for key in keys], *[in_vmem(array) for array in held])


def stage_kernel(count, *refs):
    sources, targets, sems = refs[:count], refs[count : 2 * count], refs[2 * count]
    copies = [pltpu.make_async_copy(sources[i], targets[i], sems.at[i]) for i in range(count)]
    for copy in copies:
        copy.start()
    for copy in copies:
        copy.wait()


def stage(arrays):
    count = len(arrays)
    size = sum(array.size * array.dtype.itemsize for array in arrays)
    return pl.pallas_call(
        functools.partial(stage_kernel, count),
        out_shape=tuple(jax.ShapeDtypeStruct(array.shape, array.dtype) for array in arrays),
        in_specs=[pl.BlockSpec(memory_space=pltpu.HBM)] * count,
        out_specs=(pl.BlockSpec(memory_space=pltpu.VMEM),) * count,
        scratch_shapes=[pltpu.SemaphoreType.DMA((count,))],
        compiler_params=pltpu.CompilerParams(vmem_limit_bytes=16 * 1024 * 1024),
        cost_estimate=pl.CostEstimate(flops=0, bytes_accessed=2 * size, transcendentals=0),
        name="stage",
    )(*[in_hbm(array) for array in arrays])


def gather_images(table, parts, held):
    other = lax.ppermute(pick(table, parts, 4, held), "mp", [(0, 1), (1, 0)])
    return pick(table, parts, 0, held), other


def norm_last(rows, gain):
    average = jnp.mean(rows, axis=-1, keepdims=True)
    centered = rows - average
    variance = jnp.mean(centered * centered, axis=-1, keepdims=True)
    return centered * lax.rsqrt(variance + EPS) * gain


def decode_kernel(tokens, table, *refs):
    (mine, theirs, gain_q, gain_c, gain_h, bias_h, wp) = refs[:7]
    wq, wk, wv, wo, wh = refs[7:12]
    outs = refs[12:-8]
    (xq, xc, res, q, k, v, att, hid) = refs[-8:]
    rows, half = mine.shape[1], mine.shape[2]
    views, padded, width = q.shape
    core = table[3, 0]

    for out in outs:
        out[...] = jnp.zeros_like(out)
    tail = jnp.zeros((views, padded - rows, width), BF16)
    xq[:, rows:, :] = tail
    xc[:, rows:, :] = tail
    res[:, rows:, :] = tail

    here = pl.ds(pl.multiple_of(core * half, half), half)
    there = pl.ds(pl.multiple_of((1 - core) * half, half), half)
    context_of = (1, 0, None, 2) if views == 3 else (1, 0, 3, 2)
    for j in range(4):
        raw_a, raw_b = mine[j], theirs[j]
        a, b = raw_a.astype(F32), raw_b.astype(F32)
        average = (
            jnp.sum(a, axis=-1, keepdims=True) + jnp.sum(b, axis=-1, keepdims=True)
        ) / width
        a, b = a - average, b - average
        variance = (
            jnp.sum(a * a, axis=-1, keepdims=True) + jnp.sum(b * b, axis=-1, keepdims=True)
        ) / width
        scale = lax.rsqrt(variance + EPS)
        a, b = a * scale, b * scale
        if j < views:
            xq[j, :rows, here] = (a * gain_q[:, here]).astype(BF16)
            xq[j, :rows, there] = (b * gain_q[:, there]).astype(BF16)
            res[j, :rows, here] = raw_a
            res[j, :rows, there] = raw_b
        if context_of[j] is not None:
            xc[context_of[j], :rows, here] = (a * gain_c[:, here]).astype(BF16)
            xc[context_of[j], :rows, there] = (b * gain_c[:, there]).astype(BF16)

    total = views * padded
    head_size = width // HEADS
    queries = xq[...].reshape(total, width)
    contexts = xc[...].reshape(total, width)
    proj = jnp.dot(queries, wq[...], preferred_element_type=F32)
    q[...] = (proj.astype(BF16) * BF16(head_size**-0.5)).reshape(views, padded, width)
    proj = jnp.dot(contexts, wk[...], preferred_element_type=F32)
    k[...] = proj.astype(BF16).reshape(views, padded, width)
    proj = jnp.dot(contexts, wv[...], preferred_element_type=F32)
    v[...] = proj.astype(BF16).reshape(views, padded, width)

    block = 2 * head_size
    low = lax.broadcasted_iota(jnp.int32, (padded, block), 1) < head_size
    hide = jnp.where(lax.broadcasted_iota(jnp.int32, (1, padded), 1) < tokens, 0.0, -1e30)
    nothing = jnp.zeros((padded, block), BF16)

    def attend(i, carry):
        for b in range(width // block):
            cols = slice(b * block, (b + 1) * block)
            qb, kb, vb = q[i, :, cols], k[i, :, cols], v[i, :, cols]
            qh = jnp.concatenate([jnp.where(low, qb, nothing), jnp.where(low, nothing, qb)], axis=0)
            scores = lax.dot_general(
                qh, kb, (((1,), (1,)), ((), ())), preferred_element_type=F32
            )
            scores = scores + hide
            peak = jnp.max(scores, axis=-1, keepdims=True)
            expo = jnp.exp(scores - peak)
            inverse = 1.0 / jnp.sum(expo, axis=-1, keepdims=True)
            probs = (expo * inverse).astype(BF16)
            both = jnp.dot(probs, vb, preferred_element_type=F32)
            blended = (both[:padded], both[padded:])
            att[i, :, cols] = jnp.where(low, blended[0], blended[1]).astype(BF16)
        return carry

    if views == SHARE:
        for i in range(views):
            attend(i, 0)
    else:
        lax.fori_loop(0, views, attend, 0)

    updated = jnp.dot(att[...].reshape(total, width), wo[...], preferred_element_type=F32)
    updated = updated + res[...].reshape(total, width).astype(F32)
    head_in = norm_last(updated, gain_h[...]).astype(BF16)
    hidden = jnp.dot(head_in, wh[...], preferred_element_type=F32) + bias_h[...]
    hid[...] = jax.nn.gelu(hidden).astype(BF16).reshape(views, padded, hid.shape[2])
    for i in range(views):
        raw = lax.dot_general(
            wp[...], hid[i], (((1,), (1,)), ((), ())), preferred_element_type=F32
        )
        conf = 1.0 + jnp.exp(raw[3:4])
        last = lax.broadcasted_iota(jnp.int32, raw.shape, 0) == 3
        contrib = jnp.where(last, conf, raw * conf)
        contrib = contrib[:, :tokens]
        used = table[4, i] == 1
        if len(outs) == 1:
            image = table[2, i]

            @pl.when(used)
            def _():
                outs[0][image] = outs[0][image] + contrib

            continue
        spot = table[SPOT, i]
        kept = outs[0].shape[0]

        @pl.when(jnp.logical_and(used, spot < kept))
        def _():
            outs[0][spot] = outs[0][spot] + contrib

        @pl.when(jnp.logical_and(used, spot >= kept))
        def _():
            outs[1][spot - kept] = outs[1][spot - kept] + contrib


def per_device(
    tokens,
    gain_query,
    gain_context,
    query_weight,
    key_weight,
    value_weight,
    out_weight,
    gain_head,
    hidden_weight,
    hidden_bias,
    point_weight,
    view_owner,
    view_local,
    pair_count,
):
    worker_count = lax.axis_size("pairs")
    core_count = lax.axis_size("mp")
    worker = lax.axis_index("pairs").astype(jnp.int32)
    core = lax.axis_index("mp").astype(jnp.int32)
    image_count, token_count, half = tokens.shape
    width, hidden_width = hidden_weight.shape
    rows = -(-token_count // 8) * 8
    padded = -(-token_count // 16) * 16

    shard = jnp.pad(tokens, ((0, 0), (0, rows - token_count), (0, 0)))
    scalars = pl.BlockSpec(memory_space=pltpu.SMEM)
    vector = pl.BlockSpec(memory_space=pltpu.VMEM)
    owners = view_owner[:, 0]
    weights = stage((query_weight, key_weight, value_weight, out_weight, hidden_weight))
    vectors = (
        gain_query.reshape(1, width),
        gain_context.reshape(1, width),
        gain_head.reshape(1, width),
        hidden_bias.reshape(1, hidden_width),
        point_weight,
    )

    def decode(views, spots, table, parts, vectors, weights):
        wide = pltpu.VMEM((views, padded, width), BF16)
        keep, other = gather_images(table, parts, weights)
        return pl.pallas_call(
            functools.partial(decode_kernel, token_count),
            out_shape=tuple(
                jax.ShapeDtypeStruct((count, 4, token_count), F32) for count in spots
            ),
            in_specs=[scalars] + [vector] * 12,
            out_specs=(vector,) * len(spots),
            scratch_shapes=[wide] * 7 + [pltpu.VMEM((views, padded, hidden_width), BF16)],
            compiler_params=pltpu.CompilerParams(vmem_limit_bytes=32 * 1024 * 1024),
            name="decode",
        )(table, in_vmem(keep), in_vmem(other), *vectors, *[in_vmem(w) for w in weights])

    swap = [(0, 1), (1, 0)]
    mine = image_count // core_count

    def decode_any(views, table, parts, vectors, weights):
        spots = (worker_count * image_count,)
        (flat,) = decode(views, spots, table, parts, vectors, weights)
        arrived = lax.all_to_all(flat, ("pairs", "mp"), 0, 0, tiled=True)
        return jnp.sum(arrived.reshape(worker_count * core_count, mine, 4, token_count), axis=0)

    def decode_near(views, table, parts, vectors, weights):
        spots = (3 * image_count, 2 * image_count)
        keep, send = decode(views, spots, table, parts, vectors, weights)
        leaving = keep[: 2 * image_count] + lax.ppermute(send, "mp", swap)
        order = ring_order(worker_count)
        ahead = [
            (order[i] * core_count + c, order[(i + 1 + c) % worker_count] * core_count + c)
            for i in range(worker_count)
            for c in range(core_count)
        ]
        back = [(b, a) for a, b in ahead]
        axes = ("pairs", "mp")
        total = keep[2 * image_count :] + lax.ppermute(leaving[:image_count], axes, ahead)
        total = total + lax.ppermute(leaving[image_count:], axes, back)
        theirs = lax.dynamic_slice_in_dim(total, (1 - core) * mine, mine, 0)
        ours = lax.dynamic_slice_in_dim(total, core * mine, mine, 0)
        return ours + lax.ppermute(theirs, "mp", swap)

    if worker_count == 8:
        reach = 2
        pairs = worker_count * SHARE
        table = pl.pallas_call(
            functools.partial(deal_kernel, worker_count, image_count, reach),
            out_shape=jax.ShapeDtypeStruct((SPOT + 1, 8), jnp.int32),
            in_specs=[scalars] * 4,
            out_specs=scalars,
            scratch_shapes=[pltpu.SMEM((pairs,), jnp.int32)] * 4
            + [pltpu.SMEM((worker_count,), jnp.int32)]
            + [pltpu.SMEM((worker_count * MOST,), jnp.int32)]
            + [pltpu.SMEM((worker_count,), jnp.int32)],
            compiler_params=pltpu.CompilerParams(vmem_limit_bytes=2 * 1024 * 1024),
            cost_estimate=pl.CostEstimate(flops=0, bytes_accessed=20 * 10**6, transcendentals=0),
            name="deal",
        )(owners, view_local, pair_count, jnp.stack([worker, core]))
        parts = ring_near(shard, worker_count, reach)

        def decode_far(table, near, *rest):
            return decode_any(MOST, table, ring_far(near, worker_count, reach), *rest)

        return lax.switch(
            table[LEVEL, 0],
            (
                functools.partial(decode_near, SHARE),
                functools.partial(decode_near, MOST),
                decode_far,
            ),
            table,
            parts,
            vectors,
            weights,
        )
    table = plan(owners, view_local, pair_count, worker, core, image_count, worker_count)
    parts = ring_far({0: shard, worker_count: shard}, worker_count, 0)
    return decode_any(SHARE, table, parts, vectors, weights)


def solution(mesh):
    return jax.shard_map(
        per_device,
        mesh=mesh,
        in_specs=(
            P(("groups", "pairs"), None, "mp"),
            P(),
            P(),
            P(),
            P(),
            P(),
            P(),
            P(),
            P(),
            P(),
            P(),
            P("groups", None),
            P("groups"),
            P("groups"),
        ),
        out_specs=P(("groups", "pairs", "mp"), None, None),
        check_vma=False,
    )
```

```python
import functools

import jax
import jax.numpy as jnp
from jax import lax
from jax.experimental import pallas as pl
from jax.experimental.pallas import tpu as pltpu
from jax.sharding import PartitionSpec as P

HEADS = 12
EPS = 1e-06
F32 = jnp.float32
BF16 = jnp.bfloat16


def in_hbm(array):
    return pltpu.with_memory_space_constraint(array, pltpu.HBM)


def in_vmem(array):
    return pltpu.with_memory_space_constraint(array, pltpu.VMEM)


def ring_place(index, count):
    if count > 8:
        return index
    half = index // 2
    return jnp.where(index % 2 == 0, half, count - 1 - half)


def ring_order(count):
    if count > 8:
        return list(range(count))
    return list(range(0, count, 2)) + list(range(count - 1, 0, -2))


def ring_steps(worker_count):
    order = ring_order(worker_count)
    ahead = [(order[i], order[(i + 1) % worker_count]) for i in range(worker_count)]
    return ahead, [(b, a) for a, b in ahead]


def ring_near(shard, worker_count, reach):
    ahead, back = ring_steps(worker_count)
    parts = {0: shard}
    going, coming = shard, shard
    for step in range(1, reach + 1):
        going = lax.ppermute(going, "pairs", ahead)
        coming = lax.ppermute(coming, "pairs", back)
        parts[worker_count - step] = going
        parts[step] = coming
    return parts


def ring_far(parts, worker_count, reach):
    ahead, back = ring_steps(worker_count)
    middle = worker_count // 2
    parts = dict(parts)
    going, coming = parts[worker_count - reach], parts[reach]
    half = going.shape[0] // 2
    for step in range(reach + 1, middle):
        going = lax.ppermute(going, "pairs", ahead)
        coming = lax.ppermute(coming, "pairs", back)
        parts[worker_count - step] = going
        parts[step] = coming
    parts[middle] = lax.ppermute(going[:half], "pairs", ahead)
    parts[worker_count] = lax.ppermute(coming[half:], "pairs", back)
    return parts


FIRST = (0, 1, 2, 3, 4, 5, 3, 2)
SECOND = (4, 5, 3, 2, 0, 1, 2, 3)
SHARE = 3
MOST = 4
LEVEL = 5
SPOT = 6


def deal_kernel(
    worker_count,
    image_count,
    reach,
    owners,
    locals_,
    counts,
    me,
    table,
    first,
    fits,
    holder,
    spot,
    load,
    members,
    parent,
):
    requests = owners.shape[0] // worker_count
    pairs = worker_count * SHARE
    everyone = 2**worker_count - 1

    def list_worker(w, r):
        def list_slot(s, r):
            first[r] = w * requests + 2 * s
            return r + 1

        return lax.fori_loop(0, counts[w], list_slot, r)

    lax.fori_loop(0, worker_count, list_worker, 0)

    def near(view):
        place = ring_place(owners[view], worker_count)
        turned = (2 ** (2 * reach + 1) - 1) << lax.rem(place + worker_count - reach, worker_count)
        return (turned | (turned >> worker_count)) & everyone

    def set_pair(r, carry):
        fits[r] = near(first[r]) & near(first[r] + 1)
        holder[r] = -1
        spot[r] = 0
        return carry

    lax.fori_loop(0, pairs, set_pair, 0)
    for w in range(worker_count):
        load[w] = 0
        for x in range(MOST):
            members[w * MOST + x] = 0

    def put(pair, w, slot):
        members[w * MOST + slot] = pair
        holder[pair] = w
        spot[pair] = slot

    def match(most, r):
        for w in range(worker_count):
            parent[w] = r

        def searching(state):
            seen, done, found = state
            return jnp.logical_and(found < 0, (seen & ~done) != 0)

        def search(state):
            seen, done, found = state
            todo = seen & ~done
            w = jnp.int32(0)
            for x in range(worker_count - 1, -1, -1):
                w = jnp.where(((todo >> x) & 1) == 1, jnp.int32(x), w)
            room = load[w] < most
            fresh_all = jnp.int32(0)
            for i in range(most):
                q = jnp.where(room, r, members[w * MOST + i])
                fresh = jnp.where(room, 0, fits[q] & ~(seen | fresh_all))
                for x in range(worker_count):

                    @pl.when(((fresh >> x) & 1) == 1)
                    def _():
                        parent[x] = q

                fresh_all = fresh_all | fresh
            return seen | fresh_all, done | (1 << w), jnp.where(room, w, found)

        start = (fits[r], jnp.int32(0), jnp.int32(-1))
        _, _, found = lax.while_loop(searching, search, start)

        @pl.when(found >= 0)
        def _():
            def moving(state):
                return state[0] >= 0

            def move(state):
                w, slot = state
                pair = parent[w]
                after = (holder[pair], spot[pair])
                put(pair, w, slot)
                return after

            slot = load[found]
            load[found] = slot + 1
            lax.while_loop(moving, move, (found, slot))

        return jnp.where(found < 0, 1, 0)

    missed = lax.fori_loop(0, pairs, lambda r, m: m + match(SHARE, r), jnp.int32(0))
    table[LEVEL, 0] = jnp.where(missed > 0, 1, 0)

    @pl.when(missed > 0)
    def _():
        def again(r, left):
            lost = jnp.where(holder[r] < 0, 1, 0)

            @pl.when(lost == 1)
            def _():
                match(MOST, r)

            return left + jnp.where(holder[r] < 0, 1, 0)

        left = lax.fori_loop(0, pairs, again, jnp.int32(0))

        @pl.when(left > 0)
        def _():
            table[LEVEL, 0] = 2

            def place_pair(r, carry):
                def try_worker(w, carry):
                    @pl.when(jnp.logical_and(holder[r] < 0, load[w] < MOST))
                    def _():
                        put(r, w, load[w])
                        load[w] = load[w] + 1

                    return carry

                return lax.fori_loop(0, worker_count, try_worker, carry)

            lax.fori_loop(0, pairs, place_pair, 0)

    core = me[1]
    here = ring_place(me[0], worker_count)
    middle, half = worker_count // 2, image_count // 2
    narrow = table[LEVEL, 0] == 0
    for column in range(8):
        place = jnp.where(core == 0, FIRST[column], SECOND[column])
        wide_place = jnp.where(core == 0, column, (column + 4) % 8)
        place = jnp.where(narrow, place, wide_place)
        slot = place // 2
        used = slot < load[here]
        view = first[members[here * MOST + slot]] + lax.rem(place, 2)
        owner, row = owners[view], locals_[view]
        gap = lax.rem(ring_place(owner, worker_count) - here + worker_count, worker_count)
        late = jnp.logical_and(gap == middle, row >= half)
        part = jnp.where(late, worker_count, gap)
        table[0, column] = jnp.where(used, part, 0)
        table[1, column] = jnp.where(used, jnp.where(late, row - half, row), 0)
        table[2, column] = owner * image_count + row
        table[3, column] = core
        table[4, column] = jnp.where(used, 1, 0)
        ahead = jnp.logical_or(gap == 1, gap == 2)
        nearest = jnp.logical_or(gap == 1, gap == worker_count - 1)
        ours = nearest == (core == 0)
        spot_there = jnp.where(ours, 0, 12) + jnp.where(ahead, 0, image_count) + row
        table[SPOT, column] = jnp.where(gap == 0, 2 * image_count + row, spot_there)


def plan(owners, locals_, counts, worker, core, image_count, worker_count):
    requests = locals_.shape[0] // worker_count
    share = requests // 4
    place = jnp.where(core == 0, jnp.array(FIRST, jnp.int32), jnp.array(SECOND, jnp.int32))
    pair = worker * share + place // 2
    workers = jnp.arange(worker_count, dtype=jnp.int32)
    upto = jnp.sum(
        jnp.where(workers[None, :] <= workers[:, None], counts[None, :], 0), axis=1
    )
    past = upto[None, :] <= pair[:, None]
    holder = jnp.sum(past.astype(jnp.int32), axis=1)
    slot = pair - jnp.sum(jnp.where(past, counts[None, :], 0), axis=1)
    view = holder * requests + slot * 2 + place % 2
    all_images = owners * image_count + locals_
    ids = jnp.arange(all_images.shape[0], dtype=jnp.int32)
    image = jnp.sum(jnp.where(view[:, None] == ids[None, :], all_images[None, :], 0), axis=1)
    owner, row = image // image_count, image % image_count
    gap = (ring_place(owner, worker_count) - ring_place(worker, worker_count)) % worker_count
    middle, half = worker_count // 2, image_count // 2
    late = jnp.logical_and(gap == middle, row >= half)
    part = jnp.where(late, worker_count, gap)
    row = jnp.where(late, row - half, row)
    head = jnp.broadcast_to(jnp.asarray(core, jnp.int32), (8,))
    return jnp.stack([part, row, image, head, jnp.ones_like(image)])


def fetch(table, column, keys, parts, target, sem, wait):
    if wait:
        pltpu.make_async_copy(parts[0].at[0], target, sem).wait()
        return
    part, row = table[0, column], table[1, column]
    for key, source in zip(keys, parts, strict=True):

        @pl.when(part == key)
        def _():
            pltpu.make_async_copy(source.at[row], target, sem).start()


def pick_kernel(keys, first_column, table, *refs):
    parts, (out, sems) = refs[: len(keys)], refs[-2:]
    for wait in (False, True):
        for j in range(4):
            fetch(table, first_column + j, keys, parts, out.at[j], sems.at[j], wait)


def pick(table, parts, first_column, held):
    keys = sorted(parts)
    hold = in_vmem if len(keys) < 10 else in_hbm
    space = pltpu.VMEM if len(keys) < 10 else pltpu.HBM
    _, rows, half = parts[0].shape
    return pl.pallas_call(
        functools.partial(pick_kernel, keys, first_column),
        out_shape=jax.ShapeDtypeStruct((4, rows, half), BF16),
        in_specs=[pl.BlockSpec(memory_space=pltpu.SMEM)]
        + [pl.BlockSpec(memory_space=space)] * len(keys)
        + [pl.BlockSpec(memory_space=pltpu.VMEM)] * len(held),
        out_specs=pl.BlockSpec(memory_space=pl.ANY),
        scratch_shapes=[pltpu.SemaphoreType.DMA((4,))],
        compiler_params=pltpu.CompilerParams(vmem_limit_bytes=8 * 1024 * 1024),
        cost_estimate=pl.CostEstimate(
            flops=0, bytes_accessed=16 * rows * half, transcendentals=0
        ),
        name="pick",
    )(table, *[hold(parts[key]) for key in keys], *[in_vmem(array) for array in held])


def stage_kernel(count, *refs):
    sources, targets, sems = refs[:count], refs[count : 2 * count], refs[2 * count]
    copies = [pltpu.make_async_copy(sources[i], targets[i], sems.at[i]) for i in range(count)]
    for copy in copies:
        copy.start()
    for copy in copies:
        copy.wait()


def stage(arrays):
    count = len(arrays)
    size = sum(array.size * array.dtype.itemsize for array in arrays)
    return pl.pallas_call(
        functools.partial(stage_kernel, count),
        out_shape=tuple(jax.ShapeDtypeStruct(array.shape, array.dtype) for array in arrays),
        in_specs=[pl.BlockSpec(memory_space=pltpu.HBM)] * count,
        out_specs=(pl.BlockSpec(memory_space=pltpu.VMEM),) * count,
        scratch_shapes=[pltpu.SemaphoreType.DMA((count,))],
        compiler_params=pltpu.CompilerParams(vmem_limit_bytes=16 * 1024 * 1024),
        cost_estimate=pl.CostEstimate(flops=0, bytes_accessed=2 * size, transcendentals=0),
        name="stage",
    )(*[in_hbm(array) for array in arrays])


def gather_images(table, parts, held):
    other = lax.ppermute(pick(table, parts, 4, held), "mp", [(0, 1), (1, 0)])
    return pick(table, parts, 0, held), other


def norm_last(rows, gain):
    average = jnp.mean(rows, axis=-1, keepdims=True)
    centered = rows - average
    variance = jnp.mean(centered * centered, axis=-1, keepdims=True)
    return centered * lax.rsqrt(variance + EPS) * gain


def decode_kernel(tokens, table, *refs):
    (mine, theirs, gain_q, gain_c, gain_h, bias_h, wp) = refs[:7]
    wq, wk, wv, wo, wh = refs[7:12]
    outs = refs[12:-8]
    (xq, xc, res, q, k, v, att, hid) = refs[-8:]
    rows, half = mine.shape[1], mine.shape[2]
    views, padded, width = q.shape
    core = table[3, 0]

    for out in outs:
        out[...] = jnp.zeros_like(out)
    tail = jnp.zeros((views, padded - rows, width), BF16)
    xq[:, rows:, :] = tail
    xc[:, rows:, :] = tail
    res[:, rows:, :] = tail

    here = pl.ds(pl.multiple_of(core * half, half), half)
    there = pl.ds(pl.multiple_of((1 - core) * half, half), half)
    context_of = (1, 0, None, 2) if views == 3 else (1, 0, 3, 2)
    for j in range(4):
        raw_a, raw_b = mine[j], theirs[j]
        a, b = raw_a.astype(F32), raw_b.astype(F32)
        average = (
            jnp.sum(a, axis=-1, keepdims=True) + jnp.sum(b, axis=-1, keepdims=True)
        ) / width
        a, b = a - average, b - average
        variance = (
            jnp.sum(a * a, axis=-1, keepdims=True) + jnp.sum(b * b, axis=-1, keepdims=True)
        ) / width
        scale = lax.rsqrt(variance + EPS)
        a, b = a * scale, b * scale
        if j < views:
            xq[j, :rows, here] = (a * gain_q[:, here]).astype(BF16)
            xq[j, :rows, there] = (b * gain_q[:, there]).astype(BF16)
            res[j, :rows, here] = raw_a
            res[j, :rows, there] = raw_b
        if context_of[j] is not None:
            xc[context_of[j], :rows, here] = (a * gain_c[:, here]).astype(BF16)
            xc[context_of[j], :rows, there] = (b * gain_c[:, there]).astype(BF16)

    total = views * padded
    head_size = width // HEADS
    queries = xq[...].reshape(total, width)
    contexts = xc[...].reshape(total, width)
    proj = jnp.dot(queries, wq[...], preferred_element_type=F32)
    q[...] = (proj.astype(BF16) * BF16(head_size**-0.5)).reshape(views, padded, width)
    proj = jnp.dot(contexts, wk[...], preferred_element_type=F32)
    k[...] = proj.astype(BF16).reshape(views, padded, width)
    proj = jnp.dot(contexts, wv[...], preferred_element_type=F32)
    v[...] = proj.astype(BF16).reshape(views, padded, width)

    block = 2 * head_size
    low = lax.broadcasted_iota(jnp.int32, (padded, block), 1) < head_size
    hide = jnp.where(lax.broadcasted_iota(jnp.int32, (1, padded), 1) < tokens, 0.0, -1e30)
    nothing = jnp.zeros((padded, block), BF16)

    def attend(i, carry):
        for b in range(width // block):
            cols = slice(b * block, (b + 1) * block)
            qb, kb, vb = q[i, :, cols], k[i, :, cols], v[i, :, cols]
            qh = jnp.concatenate([jnp.where(low, qb, nothing), jnp.where(low, nothing, qb)], axis=0)
            scores = lax.dot_general(
                qh, kb, (((1,), (1,)), ((), ())), preferred_element_type=F32
            )
            scores = scores + hide
            peak = jnp.max(scores, axis=-1, keepdims=True)
            expo = jnp.exp(scores - peak)
            inverse = 1.0 / jnp.sum(expo, axis=-1, keepdims=True)
            probs = (expo * inverse).astype(BF16)
            both = jnp.dot(probs, vb, preferred_element_type=F32)
            blended = (both[:padded], both[padded:])
            att[i, :, cols] = jnp.where(low, blended[0], blended[1]).astype(BF16)
        return carry

    if views == SHARE:
        for i in range(views):
            attend(i, 0)
    else:
        lax.fori_loop(0, views, attend, 0)

    updated = jnp.dot(att[...].reshape(total, width), wo[...], preferred_element_type=F32)
    updated = updated + res[...].reshape(total, width).astype(F32)
    head_in = norm_last(updated, gain_h[...]).astype(BF16)
    hidden = jnp.dot(head_in, wh[...], preferred_element_type=F32) + bias_h[...]
    hid[...] = jax.nn.gelu(hidden).astype(BF16).reshape(views, padded, hid.shape[2])
    for i in range(views):
        raw = lax.dot_general(
            wp[...], hid[i], (((1,), (1,)), ((), ())), preferred_element_type=F32
        )
        conf = 1.0 + jnp.exp(raw[3:4])
        last = lax.broadcasted_iota(jnp.int32, raw.shape, 0) == 3
        contrib = jnp.where(last, conf, raw * conf)
        contrib = contrib[:, :tokens]
        used = table[4, i] == 1
        if len(outs) == 1:
            image = table[2, i]

            @pl.when(used)
            def _():
                outs[0][image] = outs[0][image] + contrib

            continue
        spot = table[SPOT, i]
        kept = outs[0].shape[0]

        @pl.when(jnp.logical_and(used, spot < kept))
        def _():
            outs[0][spot] = outs[0][spot] + contrib

        @pl.when(jnp.logical_and(used, spot >= kept))
        def _():
            outs[1][spot - kept] = outs[1][spot - kept] + contrib


def per_device(
    tokens,
    gain_query,
    gain_context,
    query_weight,
    key_weight,
    value_weight,
    out_weight,
    gain_head,
    hidden_weight,
    hidden_bias,
    point_weight,
    view_owner,
    view_local,
    pair_count,
):
    worker_count = lax.axis_size("pairs")
    core_count = lax.axis_size("mp")
    worker = lax.axis_index("pairs").astype(jnp.int32)
    core = lax.axis_index("mp").astype(jnp.int32)
    image_count, token_count, half = tokens.shape
    width, hidden_width = hidden_weight.shape
    rows = -(-token_count // 8) * 8
    padded = -(-token_count // 16) * 16

    shard = jnp.pad(tokens, ((0, 0), (0, rows - token_count), (0, 0)))
    scalars = pl.BlockSpec(memory_space=pltpu.SMEM)
    vector = pl.BlockSpec(memory_space=pltpu.VMEM)
    owners = view_owner[:, 0]
    weights = stage((query_weight, key_weight, value_weight, out_weight, hidden_weight))
    vectors = (
        gain_query.reshape(1, width),
        gain_context.reshape(1, width),
        gain_head.reshape(1, width),
        hidden_bias.reshape(1, hidden_width),
        point_weight,
    )

    def decode(views, spots, table, parts, vectors, weights):
        wide = pltpu.VMEM((views, padded, width), BF16)
        keep, other = gather_images(table, parts, weights)
        return pl.pallas_call(
            functools.partial(decode_kernel, token_count),
            out_shape=tuple(
                jax.ShapeDtypeStruct((count, 4, token_count), F32) for count in spots
            ),
            in_specs=[scalars] + [vector] * 12,
            out_specs=(vector,) * len(spots),
            scratch_shapes=[wide] * 7 + [pltpu.VMEM((views, padded, hidden_width), BF16)],
            compiler_params=pltpu.CompilerParams(vmem_limit_bytes=32 * 1024 * 1024),
            name="decode",
        )(table, in_vmem(keep), in_vmem(other), *vectors, *[in_vmem(w) for w in weights])

    swap = [(0, 1), (1, 0)]
    mine = image_count // core_count

    def decode_any(views, table, parts, vectors, weights):
        spots = (worker_count * image_count,)
        (flat,) = decode(views, spots, table, parts, vectors, weights)
        arrived = lax.all_to_all(flat, ("pairs", "mp"), 0, 0, tiled=True)
        return jnp.sum(arrived.reshape(worker_count * core_count, mine, 4, token_count), axis=0)

    def decode_near(views, table, parts, vectors, weights):
        spots = (3 * image_count, 2 * image_count)
        keep, send = decode(views, spots, table, parts, vectors, weights)
        leaving = keep[: 2 * image_count] + lax.ppermute(send, "mp", swap)
        order = ring_order(worker_count)
        ahead = [
            (order[i] * core_count + c, order[(i + 1 + c) % worker_count] * core_count + c)
            for i in range(worker_count)
            for c in range(core_count)
        ]
        back = [(b, a) for a, b in ahead]
        axes = ("pairs", "mp")
        total = keep[2 * image_count :] + lax.ppermute(leaving[:image_count], axes, ahead)
        total = total + lax.ppermute(leaving[image_count:], axes, back)
        theirs = lax.dynamic_slice_in_dim(total, (1 - core) * mine, mine, 0)
        ours = lax.dynamic_slice_in_dim(total, core * mine, mine, 0)
        return ours + lax.ppermute(theirs, "mp", swap)

    if worker_count == 8:
        reach = 2
        pairs = worker_count * SHARE
        table = pl.pallas_call(
            functools.partial(deal_kernel, worker_count, image_count, reach),
            out_shape=jax.ShapeDtypeStruct((SPOT + 1, 8), jnp.int32),
            in_specs=[scalars] * 4,
            out_specs=scalars,
            scratch_shapes=[pltpu.SMEM((pairs,), jnp.int32)] * 4
            + [pltpu.SMEM((worker_count,), jnp.int32)]
            + [pltpu.SMEM((worker_count * MOST,), jnp.int32)]
            + [pltpu.SMEM((worker_count,), jnp.int32)],
            compiler_params=pltpu.CompilerParams(vmem_limit_bytes=2 * 1024 * 1024),
            cost_estimate=pl.CostEstimate(flops=0, bytes_accessed=20 * 10**6, transcendentals=0),
            name="deal",
        )(owners, view_local, pair_count, jnp.stack([worker, core]))
        parts = ring_near(shard, worker_count, reach)

        def decode_far(table, near, *rest):
            return decode_any(MOST, table, ring_far(near, worker_count, reach), *rest)

        return lax.switch(
            table[LEVEL, 0],
            (
                functools.partial(decode_near, SHARE),
                functools.partial(decode_near, MOST),
                decode_far,
            ),
            table,
            parts,
            vectors,
            weights,
        )
    table = plan(owners, view_local, pair_count, worker, core, image_count, worker_count)
    parts = ring_far({0: shard, worker_count: shard}, worker_count, 0)
    return decode_any(SHARE, table, parts, vectors, weights)


def solution(mesh):
    return jax.shard_map(
        per_device,
        mesh=mesh,
        in_specs=(
            P(("groups", "pairs"), None, "mp"),
            P(),
            P(),
            P(),
            P(),
            P(),
            P(),
            P(),
            P(),
            P(),
            P(),
            P("groups", None),
            P("groups"),
            P("groups"),
        ),
        out_specs=P(("groups", "pairs", "mp"), None, None),
        check_vma=False,
    )
```

```python
import functools

import jax
import jax.numpy as jnp
from jax import lax
from jax.experimental import pallas as pl
from jax.experimental.pallas import tpu as pltpu
from jax.sharding import PartitionSpec as P

HEADS = 12
EPS = 1e-06
F32 = jnp.float32
BF16 = jnp.bfloat16


def in_hbm(array):
    return pltpu.with_memory_space_constraint(array, pltpu.HBM)


def in_vmem(array):
    return pltpu.with_memory_space_constraint(array, pltpu.VMEM)


def ring_place(index, count):
    if count > 8:
        return index
    half = index // 2
    return jnp.where(index % 2 == 0, half, count - 1 - half)


def ring_order(count):
    if count > 8:
        return list(range(count))
    return list(range(0, count, 2)) + list(range(count - 1, 0, -2))


def ring_steps(worker_count):
    order = ring_order(worker_count)
    ahead = [(order[i], order[(i + 1) % worker_count]) for i in range(worker_count)]
    return ahead, [(b, a) for a, b in ahead]


def ring_near(shard, worker_count, reach):
    ahead, back = ring_steps(worker_count)
    parts = {0: shard}
    going, coming = shard, shard
    for step in range(1, reach + 1):
        going = lax.ppermute(going, "pairs", ahead)
        coming = lax.ppermute(coming, "pairs", back)
        parts[worker_count - step] = going
        parts[step] = coming
    return parts


def ring_far(parts, worker_count, reach):
    ahead, back = ring_steps(worker_count)
    middle = worker_count // 2
    parts = dict(parts)
    going, coming = parts[worker_count - reach], parts[reach]
    half = going.shape[0] // 2
    for step in range(reach + 1, middle):
        going = lax.ppermute(going, "pairs", ahead)
        coming = lax.ppermute(coming, "pairs", back)
        parts[worker_count - step] = going
        parts[step] = coming
    parts[middle] = lax.ppermute(going[:half], "pairs", ahead)
    parts[worker_count] = lax.ppermute(coming[half:], "pairs", back)
    return parts


FIRST = (0, 1, 2, 3, 4, 5, 3, 2)
SECOND = (4, 5, 3, 2, 0, 1, 2, 3)
SHARE = 3
MOST = 4
LEVEL = 5
SPOT = 6


def deal_kernel(
    worker_count,
    image_count,
    reach,
    owners,
    locals_,
    counts,
    me,
    table,
    first,
    fits,
    holder,
    spot,
    load,
    members,
    parent,
):
    requests = owners.shape[0] // worker_count
    pairs = worker_count * SHARE
    everyone = 2**worker_count - 1

    def list_worker(w, r):
        def list_slot(s, r):
            first[r] = w * requests + 2 * s
            return r + 1

        return lax.fori_loop(0, counts[w], list_slot, r)

    lax.fori_loop(0, worker_count, list_worker, 0)

    def near(view):
        place = ring_place(owners[view], worker_count)
        turned = (2 ** (2 * reach + 1) - 1) << lax.rem(place + worker_count - reach, worker_count)
        return (turned | (turned >> worker_count)) & everyone

    def set_pair(r, carry):
        fits[r] = near(first[r]) & near(first[r] + 1)
        holder[r] = -1
        spot[r] = 0
        return carry

    lax.fori_loop(0, pairs, set_pair, 0)
    for w in range(worker_count):
        load[w] = 0
        for x in range(MOST):
            members[w * MOST + x] = 0

    def put(pair, w, slot):
        members[w * MOST + slot] = pair
        holder[pair] = w
        spot[pair] = slot

    def match(most, r):
        for w in range(worker_count):
            parent[w] = r

        def searching(state):
            seen, done, found = state
            return jnp.logical_and(found < 0, (seen & ~done) != 0)

        def search(state):
            seen, done, found = state
            todo = seen & ~done
            w = jnp.int32(0)
            for x in range(worker_count - 1, -1, -1):
                w = jnp.where(((todo >> x) & 1) == 1, jnp.int32(x), w)
            room = load[w] < most
            fresh_all = jnp.int32(0)
            for i in range(most):
                q = jnp.where(room, r, members[w * MOST + i])
                fresh = jnp.where(room, 0, fits[q] & ~(seen | fresh_all))
                for x in range(worker_count):

                    @pl.when(((fresh >> x) & 1) == 1)
                    def _():
                        parent[x] = q

                fresh_all = fresh_all | fresh
            return seen | fresh_all, done | (1 << w), jnp.where(room, w, found)

        start = (fits[r], jnp.int32(0), jnp.int32(-1))
        _, _, found = lax.while_loop(searching, search, start)

        @pl.when(found >= 0)
        def _():
            def moving(state):
                return state[0] >= 0

            def move(state):
                w, slot = state
                pair = parent[w]
                after = (holder[pair], spot[pair])
                put(pair, w, slot)
                return after

            slot = load[found]
            load[found] = slot + 1
            lax.while_loop(moving, move, (found, slot))

        return jnp.where(found < 0, 1, 0)

    missed = lax.fori_loop(0, pairs, lambda r, m: m + match(SHARE, r), jnp.int32(0))
    table[LEVEL, 0] = jnp.where(missed > 0, 1, 0)

    @pl.when(missed > 0)
    def _():
        def again(r, left):
            lost = jnp.where(holder[r] < 0, 1, 0)

            @pl.when(lost == 1)
            def _():
                match(MOST, r)

            return left + jnp.where(holder[r] < 0, 1, 0)

        left = lax.fori_loop(0, pairs, again, jnp.int32(0))

        @pl.when(left > 0)
        def _():
            table[LEVEL, 0] = 2

            def place_pair(r, carry):
                def try_worker(w, carry):
                    @pl.when(jnp.logical_and(holder[r] < 0, load[w] < MOST))
                    def _():
                        put(r, w, load[w])
                        load[w] = load[w] + 1

                    return carry

                return lax.fori_loop(0, worker_count, try_worker, carry)

            lax.fori_loop(0, pairs, place_pair, 0)

    core = me[1]
    here = ring_place(me[0], worker_count)
    middle, half = worker_count // 2, image_count // 2
    narrow = table[LEVEL, 0] == 0
    for column in range(8):
        place = jnp.where(core == 0, FIRST[column], SECOND[column])
        wide_place = jnp.where(core == 0, column, (column + 4) % 8)
        place = jnp.where(narrow, place, wide_place)
        slot = place // 2
        used = slot < load[here]
        view = first[members[here * MOST + slot]] + lax.rem(place, 2)
        owner, row = owners[view], locals_[view]
        gap = lax.rem(ring_place(owner, worker_count) - here + worker_count, worker_count)
        late = jnp.logical_and(gap == middle, row >= half)
        part = jnp.where(late, worker_count, gap)
        table[0, column] = jnp.where(used, part, 0)
        table[1, column] = jnp.where(used, jnp.where(late, row - half, row), 0)
        table[2, column] = owner * image_count + row
        table[3, column] = core
        table[4, column] = jnp.where(used, 1, 0)
        ahead = jnp.logical_or(gap == 1, gap == 2)
        nearest = jnp.logical_or(gap == 1, gap == worker_count - 1)
        ours = nearest == (core == 0)
        spot_there = jnp.where(ours, 0, 12) + jnp.where(ahead, 0, image_count) + row
        table[SPOT, column] = jnp.where(gap == 0, 2 * image_count + row, spot_there)


def plan(owners, locals_, counts, worker, core, image_count, worker_count):
    requests = locals_.shape[0] // worker_count
    share = requests // 4
    place = jnp.where(core == 0, jnp.array(FIRST, jnp.int32), jnp.array(SECOND, jnp.int32))
    pair = worker * share + place // 2
    workers = jnp.arange(worker_count, dtype=jnp.int32)
    upto = jnp.sum(
        jnp.where(workers[None, :] <= workers[:, None], counts[None, :], 0), axis=1
    )
    past = upto[None, :] <= pair[:, None]
    holder = jnp.sum(past.astype(jnp.int32), axis=1)
    slot = pair - jnp.sum(jnp.where(past, counts[None, :], 0), axis=1)
    view = holder * requests + slot * 2 + place % 2
    all_images = owners * image_count + locals_
    ids = jnp.arange(all_images.shape[0], dtype=jnp.int32)
    image = jnp.sum(jnp.where(view[:, None] == ids[None, :], all_images[None, :], 0), axis=1)
    owner, row = image // image_count, image % image_count
    gap = (ring_place(owner, worker_count) - ring_place(worker, worker_count)) % worker_count
    middle, half = worker_count // 2, image_count // 2
    late = jnp.logical_and(gap == middle, row >= half)
    part = jnp.where(late, worker_count, gap)
    row = jnp.where(late, row - half, row)
    head = jnp.broadcast_to(jnp.asarray(core, jnp.int32), (8,))
    return jnp.stack([part, row, image, head, jnp.ones_like(image)])


def fetch(table, column, keys, parts, target, sem, wait):
    if wait:
        pltpu.make_async_copy(parts[0].at[0], target, sem).wait()
        return
    part, row = table[0, column], table[1, column]
    for key, source in zip(keys, parts, strict=True):

        @pl.when(part == key)
        def _():
            pltpu.make_async_copy(source.at[row], target, sem).start()


def pick_kernel(keys, first_column, table, *refs):
    parts, (out, sems) = refs[: len(keys)], refs[-2:]
    for wait in (False, True):
        for j in range(4):
            fetch(table, first_column + j, keys, parts, out.at[j], sems.at[j], wait)


def pick(table, parts, first_column, held):
    keys = sorted(parts)
    hold = in_vmem if len(keys) < 10 else in_hbm
    space = pltpu.VMEM if len(keys) < 10 else pltpu.HBM
    _, rows, half = parts[0].shape
    return pl.pallas_call(
        functools.partial(pick_kernel, keys, first_column),
        out_shape=jax.ShapeDtypeStruct((4, rows, half), BF16),
        in_specs=[pl.BlockSpec(memory_space=pltpu.SMEM)]
        + [pl.BlockSpec(memory_space=space)] * len(keys)
        + [pl.BlockSpec(memory_space=pltpu.VMEM)] * len(held),
        out_specs=pl.BlockSpec(memory_space=pl.ANY),
        scratch_shapes=[pltpu.SemaphoreType.DMA((4,))],
        compiler_params=pltpu.CompilerParams(vmem_limit_bytes=8 * 1024 * 1024),
        cost_estimate=pl.CostEstimate(
            flops=0, bytes_accessed=16 * rows * half, transcendentals=0
        ),
        name="pick",
    )(table, *[hold(parts[key]) for key in keys], *[in_vmem(array) for array in held])


def stage_kernel(count, *refs):
    sources, targets, sems = refs[:count], refs[count : 2 * count], refs[2 * count]
    copies = [pltpu.make_async_copy(sources[i], targets[i], sems.at[i]) for i in range(count)]
    for copy in copies:
        copy.start()
    for copy in copies:
        copy.wait()


def stage(arrays):
    count = len(arrays)
    size = sum(array.size * array.dtype.itemsize for array in arrays)
    return pl.pallas_call(
        functools.partial(stage_kernel, count),
        out_shape=tuple(jax.ShapeDtypeStruct(array.shape, array.dtype) for array in arrays),
        in_specs=[pl.BlockSpec(memory_space=pltpu.HBM)] * count,
        out_specs=(pl.BlockSpec(memory_space=pltpu.VMEM),) * count,
        scratch_shapes=[pltpu.SemaphoreType.DMA((count,))],
        compiler_params=pltpu.CompilerParams(vmem_limit_bytes=16 * 1024 * 1024),
        cost_estimate=pl.CostEstimate(flops=0, bytes_accessed=2 * size, transcendentals=0),
        name="stage",
    )(*[in_hbm(array) for array in arrays])


def gather_images(table, parts, held):
    other = lax.ppermute(pick(table, parts, 4, held), "mp", [(0, 1), (1, 0)])
    return pick(table, parts, 0, held), other


def norm_last(rows, gain):
    average = jnp.mean(rows, axis=-1, keepdims=True)
    centered = rows - average
    variance = jnp.mean(centered * centered, axis=-1, keepdims=True)
    return centered * lax.rsqrt(variance + EPS) * gain


def decode_kernel(tokens, table, *refs):
    (mine, theirs, gain_q, gain_c, gain_h, bias_h, wp) = refs[:7]
    wq, wk, wv, wo, wh = refs[7:12]
    outs = refs[12:-8]
    (xq, xc, res, q, k, v, att, hid) = refs[-8:]
    rows, half = mine.shape[1], mine.shape[2]
    views, padded, width = q.shape
    core = table[3, 0]

    for out in outs:
        out[...] = jnp.zeros_like(out)
    tail = jnp.zeros((views, padded - rows, width), BF16)
    att[:, rows:, :] = tail
    res[:, rows:, :] = tail

    here = pl.ds(pl.multiple_of(core * half, half), half)
    there = pl.ds(pl.multiple_of((1 - core) * half, half), half)
    context_of = (1, 0, None, 2) if views == 3 else (1, 0, 3, 2)
    for j in range(4):
        whole, spot = (res, j) if j < views else (att, 0)
        whole[spot, :rows, here] = mine[j]
        whole[spot, :rows, there] = theirs[j]
        full = whole[spot].astype(F32)
        average = jnp.mean(full, axis=-1, keepdims=True)
        full = full - average
        variance = jnp.mean(full * full, axis=-1, keepdims=True)
        full = full * lax.rsqrt(variance + EPS)
        if j < views:
            xq[j] = (full * gain_q[...]).astype(BF16)
        if context_of[j] is not None:
            xc[context_of[j]] = (full * gain_c[...]).astype(BF16)

    total = views * padded
    head_size = width // HEADS
    queries = xq[...].reshape(total, width)
    contexts = xc[...].reshape(total, width)
    proj = jnp.dot(queries, wq[...], preferred_element_type=F32)
    q[...] = (proj.astype(BF16) * BF16(head_size**-0.5)).reshape(views, padded, width)
    proj = jnp.dot(contexts, wk[...], preferred_element_type=F32)
    k[...] = proj.astype(BF16).reshape(views, padded, width)
    proj = jnp.dot(contexts, wv[...], preferred_element_type=F32)
    v[...] = proj.astype(BF16).reshape(views, padded, width)

    block = 2 * head_size
    low = lax.broadcasted_iota(jnp.int32, (padded, block), 1) < head_size
    hide = jnp.where(lax.broadcasted_iota(jnp.int32, (1, padded), 1) < tokens, 0.0, -1e30)
    nothing = jnp.zeros((padded, block), BF16)

    def attend(i, carry):
        for b in range(width // block):
            cols = slice(b * block, (b + 1) * block)
            qb, kb, vb = q[i, :, cols], k[i, :, cols], v[i, :, cols]
            qh = jnp.concatenate([jnp.where(low, qb, nothing), jnp.where(low, nothing, qb)], axis=0)
            scores = lax.dot_general(
                qh, kb, (((1,), (1,)), ((), ())), preferred_element_type=F32
            )
            scores = scores + hide
            peak = jnp.max(scores, axis=-1, keepdims=True)
            expo = jnp.exp(scores - peak)
            inverse = 1.0 / jnp.sum(expo, axis=-1, keepdims=True)
            probs = (expo * inverse).astype(BF16)
            both = jnp.dot(probs, vb, preferred_element_type=F32)
            blended = (both[:padded], both[padded:])
            att[i, :, cols] = jnp.where(low, blended[0], blended[1]).astype(BF16)
        return carry

    if views == SHARE:
        for i in range(views):
            attend(i, 0)
    else:
        lax.fori_loop(0, views, attend, 0)

    updated = jnp.dot(att[...].reshape(total, width), wo[...], preferred_element_type=F32)
    updated = updated + res[...].reshape(total, width).astype(F32)
    head_in = norm_last(updated, gain_h[...]).astype(BF16)
    hidden = jnp.dot(head_in, wh[...], preferred_element_type=F32) + bias_h[...]
    hid[...] = jax.nn.gelu(hidden).astype(BF16).reshape(views, padded, hid.shape[2])
    for i in range(views):
        raw = lax.dot_general(
            wp[...], hid[i], (((1,), (1,)), ((), ())), preferred_element_type=F32
        )
        conf = 1.0 + jnp.exp(raw[3:4])
        last = lax.broadcasted_iota(jnp.int32, raw.shape, 0) == 3
        contrib = jnp.where(last, conf, raw * conf)
        contrib = contrib[:, :tokens]
        used = table[4, i] == 1
        if len(outs) == 1:
            image = table[2, i]

            @pl.when(used)
            def _():
                outs[0][image] = outs[0][image] + contrib

            continue
        spot = table[SPOT, i]
        kept = outs[0].shape[0]

        @pl.when(jnp.logical_and(used, spot < kept))
        def _():
            outs[0][spot] = outs[0][spot] + contrib

        @pl.when(jnp.logical_and(used, spot >= kept))
        def _():
            outs[1][spot - kept] = outs[1][spot - kept] + contrib


def per_device(
    tokens,
    gain_query,
    gain_context,
    query_weight,
    key_weight,
    value_weight,
    out_weight,
    gain_head,
    hidden_weight,
    hidden_bias,
    point_weight,
    view_owner,
    view_local,
    pair_count,
):
    worker_count = lax.axis_size("pairs")
    core_count = lax.axis_size("mp")
    worker = lax.axis_index("pairs").astype(jnp.int32)
    core = lax.axis_index("mp").astype(jnp.int32)
    image_count, token_count, half = tokens.shape
    width, hidden_width = hidden_weight.shape
    rows = -(-token_count // 8) * 8
    padded = -(-token_count // 16) * 16

    shard = jnp.pad(tokens, ((0, 0), (0, rows - token_count), (0, 0)))
    scalars = pl.BlockSpec(memory_space=pltpu.SMEM)
    vector = pl.BlockSpec(memory_space=pltpu.VMEM)
    owners = view_owner[:, 0]
    weights = stage((query_weight, key_weight, value_weight, out_weight, hidden_weight))
    vectors = (
        gain_query.reshape(1, width),
        gain_context.reshape(1, width),
        gain_head.reshape(1, width),
        hidden_bias.reshape(1, hidden_width),
        point_weight,
    )

    def decode(views, spots, table, parts, vectors, weights):
        wide = pltpu.VMEM((views, padded, width), BF16)
        keep, other = gather_images(table, parts, weights)
        return pl.pallas_call(
            functools.partial(decode_kernel, token_count),
            out_shape=tuple(
                jax.ShapeDtypeStruct((count, 4, token_count), F32) for count in spots
            ),
            in_specs=[scalars] + [vector] * 12,
            out_specs=(vector,) * len(spots),
            scratch_shapes=[wide] * 7 + [pltpu.VMEM((views, padded, hidden_width), BF16)],
            compiler_params=pltpu.CompilerParams(vmem_limit_bytes=32 * 1024 * 1024),
            name="decode",
        )(table, in_vmem(keep), in_vmem(other), *vectors, *[in_vmem(w) for w in weights])

    swap = [(0, 1), (1, 0)]
    mine = image_count // core_count

    def decode_any(views, table, parts, vectors, weights):
        spots = (worker_count * image_count,)
        (flat,) = decode(views, spots, table, parts, vectors, weights)
        arrived = lax.all_to_all(flat, ("pairs", "mp"), 0, 0, tiled=True)
        arrived = arrived.reshape(worker_count * core_count, mine, 4, token_count)
        return jnp.sum(arrived, axis=0), jnp.zeros_like(arrived[0])

    def decode_near(views, table, parts, vectors, weights):
        spots = (3 * image_count, 2 * image_count)
        keep, send = decode(views, spots, table, parts, vectors, weights)
        leaving = keep[: 2 * image_count] + lax.ppermute(send, "mp", swap)
        order = ring_order(worker_count)
        ahead = [
            (order[i] * core_count + c, order[(i + 1 + c) % worker_count] * core_count + c)
            for i in range(worker_count)
            for c in range(core_count)
        ]
        back = [(b, a) for a, b in ahead]
        axes = ("pairs", "mp")
        total = keep[2 * image_count :] + lax.ppermute(leaving[:image_count], axes, ahead)
        total = total + lax.ppermute(leaving[image_count:], axes, back)
        theirs = lax.dynamic_slice_in_dim(total, (1 - core) * mine, mine, 0)
        ours = lax.dynamic_slice_in_dim(total, core * mine, mine, 0)
        return ours, lax.ppermute(theirs, "mp", swap)

    if worker_count == 8:
        reach = 2
        pairs = worker_count * SHARE
        table = pl.pallas_call(
            functools.partial(deal_kernel, worker_count, image_count, reach),
            out_shape=jax.ShapeDtypeStruct((SPOT + 1, 8), jnp.int32),
            in_specs=[scalars] * 4,
            out_specs=scalars,
            scratch_shapes=[pltpu.SMEM((pairs,), jnp.int32)] * 4
            + [pltpu.SMEM((worker_count,), jnp.int32)]
            + [pltpu.SMEM((worker_count * MOST,), jnp.int32)]
            + [pltpu.SMEM((worker_count,), jnp.int32)],
            compiler_params=pltpu.CompilerParams(vmem_limit_bytes=2 * 1024 * 1024),
            cost_estimate=pl.CostEstimate(flops=0, bytes_accessed=20 * 10**6, transcendentals=0),
            name="deal",
        )(owners, view_local, pair_count, jnp.stack([worker, core]))
        parts = ring_near(shard, worker_count, reach)

        def decode_far(table, near, *rest):
            return decode_any(MOST, table, ring_far(near, worker_count, reach), *rest)

        ours, theirs = lax.switch(
            table[LEVEL, 0],
            (
                functools.partial(decode_near, SHARE),
                functools.partial(decode_near, MOST),
                decode_far,
            ),
            table,
            parts,
            vectors,
            weights,
        )
        return ours + theirs
    table = plan(owners, view_local, pair_count, worker, core, image_count, worker_count)
    parts = ring_far({0: shard, worker_count: shard}, worker_count, 0)
    ours, theirs = decode_any(SHARE, table, parts, vectors, weights)
    return ours + theirs


def solution(mesh):
    return jax.shard_map(
        per_device,
        mesh=mesh,
        in_specs=(
            P(("groups", "pairs"), None, "mp"),
            P(),
            P(),
            P(),
            P(),
            P(),
            P(),
            P(),
            P(),
            P(),
            P(),
            P("groups", None),
            P("groups"),
            P("groups"),
        ),
        out_specs=P(("groups", "pairs", "mp"), None, None),
        check_vma=False,
    )
```

```python
import functools

import jax
import jax.numpy as jnp
from jax import lax
from jax.experimental import pallas as pl
from jax.experimental.pallas import tpu as pltpu
from jax.sharding import PartitionSpec as P

HEADS = 12
EPS = 1e-06
F32 = jnp.float32
BF16 = jnp.bfloat16


def in_hbm(array):
    return pltpu.with_memory_space_constraint(array, pltpu.HBM)


def in_vmem(array):
    return pltpu.with_memory_space_constraint(array, pltpu.VMEM)


def ring_place(index, count):
    if count > 8:
        return index
    half = index // 2
    return jnp.where(index % 2 == 0, half, count - 1 - half)


def ring_order(count):
    if count > 8:
        return list(range(count))
    return list(range(0, count, 2)) + list(range(count - 1, 0, -2))


def ring_steps(worker_count):
    order = ring_order(worker_count)
    ahead = [(order[i], order[(i + 1) % worker_count]) for i in range(worker_count)]
    return ahead, [(b, a) for a, b in ahead]


def ring_near(shard, worker_count, reach):
    ahead, back = ring_steps(worker_count)
    parts = {0: shard}
    going, coming = shard, shard
    for step in range(1, reach + 1):
        going = lax.ppermute(going, "pairs", ahead)
        coming = lax.ppermute(coming, "pairs", back)
        parts[worker_count - step] = going
        parts[step] = coming
    return parts


def ring_far(parts, worker_count, reach):
    ahead, back = ring_steps(worker_count)
    middle = worker_count // 2
    parts = dict(parts)
    going, coming = parts[worker_count - reach], parts[reach]
    half = going.shape[0] // 2
    for step in range(reach + 1, middle):
        going = lax.ppermute(going, "pairs", ahead)
        coming = lax.ppermute(coming, "pairs", back)
        parts[worker_count - step] = going
        parts[step] = coming
    parts[middle] = lax.ppermute(going[:half], "pairs", ahead)
    parts[worker_count] = lax.ppermute(coming[half:], "pairs", back)
    return parts


FIRST = (0, 1, 2, 3, 4, 5, 3, 2)
SECOND = (4, 5, 3, 2, 0, 1, 2, 3)
SHARE = 3
MOST = 4
LEVEL = 5
SPOT = 6


def deal_kernel(
    worker_count,
    image_count,
    reach,
    owners,
    locals_,
    counts,
    me,
    table,
    first,
    fits,
    holder,
    spot,
    load,
    members,
    parent,
):
    requests = owners.shape[0] // worker_count
    pairs = worker_count * SHARE
    everyone = 2**worker_count - 1

    def list_worker(w, r):
        def list_slot(s, r):
            first[r] = w * requests + 2 * s
            return r + 1

        return lax.fori_loop(0, counts[w], list_slot, r)

    lax.fori_loop(0, worker_count, list_worker, 0)

    def near(view):
        place = ring_place(owners[view], worker_count)
        turned = (2 ** (2 * reach + 1) - 1) << lax.rem(place + worker_count - reach, worker_count)
        return (turned | (turned >> worker_count)) & everyone

    def set_pair(r, carry):
        fits[r] = near(first[r]) & near(first[r] + 1)
        holder[r] = -1
        spot[r] = 0
        return carry

    lax.fori_loop(0, pairs, set_pair, 0)
    for w in range(worker_count):
        load[w] = 0
        for x in range(MOST):
            members[w * MOST + x] = 0

    def put(pair, w, slot):
        members[w * MOST + slot] = pair
        holder[pair] = w
        spot[pair] = slot

    def match(most, r):
        for w in range(worker_count):
            parent[w] = r

        def searching(state):
            seen, done, found = state
            return jnp.logical_and(found < 0, (seen & ~done) != 0)

        def search(state):
            seen, done, found = state
            todo = seen & ~done
            w = jnp.int32(0)
            for x in range(worker_count - 1, -1, -1):
                w = jnp.where(((todo >> x) & 1) == 1, jnp.int32(x), w)
            room = load[w] < most
            fresh_all = jnp.int32(0)
            for i in range(most):
                q = jnp.where(room, r, members[w * MOST + i])
                fresh = jnp.where(room, 0, fits[q] & ~(seen | fresh_all))
                for x in range(worker_count):

                    @pl.when(((fresh >> x) & 1) == 1)
                    def _():
                        parent[x] = q

                fresh_all = fresh_all | fresh
            return seen | fresh_all, done | (1 << w), jnp.where(room, w, found)

        start = (fits[r], jnp.int32(0), jnp.int32(-1))
        _, _, found = lax.while_loop(searching, search, start)

        @pl.when(found >= 0)
        def _():
            def moving(state):
                return state[0] >= 0

            def move(state):
                w, slot = state
                pair = parent[w]
                after = (holder[pair], spot[pair])
                put(pair, w, slot)
                return after

            slot = load[found]
            load[found] = slot + 1
            lax.while_loop(moving, move, (found, slot))

        return jnp.where(found < 0, 1, 0)

    missed = lax.fori_loop(0, pairs, lambda r, m: m + match(SHARE, r), jnp.int32(0))
    table[LEVEL, 0] = jnp.where(missed > 0, 1, 0)

    @pl.when(missed > 0)
    def _():
        def again(r, left):
            lost = jnp.where(holder[r] < 0, 1, 0)

            @pl.when(lost == 1)
            def _():
                match(MOST, r)

            return left + jnp.where(holder[r] < 0, 1, 0)

        left = lax.fori_loop(0, pairs, again, jnp.int32(0))

        @pl.when(left > 0)
        def _():
            table[LEVEL, 0] = 2

            def place_pair(r, carry):
                def try_worker(w, carry):
                    @pl.when(jnp.logical_and(holder[r] < 0, load[w] < MOST))
                    def _():
                        put(r, w, load[w])
                        load[w] = load[w] + 1

                    return carry

                return lax.fori_loop(0, worker_count, try_worker, carry)

            lax.fori_loop(0, pairs, place_pair, 0)

    core = me[1]
    here = ring_place(me[0], worker_count)
    middle, half = worker_count // 2, image_count // 2
    narrow = table[LEVEL, 0] == 0
    for column in range(8):
        place = jnp.where(core == 0, FIRST[column], SECOND[column])
        wide_place = jnp.where(core == 0, column, (column + 4) % 8)
        place = jnp.where(narrow, place, wide_place)
        slot = place // 2
        used = slot < load[here]
        view = first[members[here * MOST + slot]] + lax.rem(place, 2)
        owner, row = owners[view], locals_[view]
        gap = lax.rem(ring_place(owner, worker_count) - here + worker_count, worker_count)
        late = jnp.logical_and(gap == middle, row >= half)
        part = jnp.where(late, worker_count, gap)
        table[0, column] = jnp.where(used, part, 0)
        table[1, column] = jnp.where(used, jnp.where(late, row - half, row), 0)
        table[2, column] = owner * image_count + row
        table[3, column] = core
        table[4, column] = jnp.where(used, 1, 0)
        ahead = jnp.logical_or(gap == 1, gap == 2)
        nearest = jnp.logical_or(gap == 1, gap == worker_count - 1)
        ours = nearest == (core == 0)
        spot_there = jnp.where(ours, 0, 12) + jnp.where(ahead, 0, image_count) + row
        table[SPOT, column] = jnp.where(gap == 0, 2 * image_count + row, spot_there)


def plan(owners, locals_, counts, worker, core, image_count, worker_count):
    requests = locals_.shape[0] // worker_count
    share = requests // 4
    place = jnp.where(core == 0, jnp.array(FIRST, jnp.int32), jnp.array(SECOND, jnp.int32))
    pair = worker * share + place // 2
    workers = jnp.arange(worker_count, dtype=jnp.int32)
    upto = jnp.sum(
        jnp.where(workers[None, :] <= workers[:, None], counts[None, :], 0), axis=1
    )
    past = upto[None, :] <= pair[:, None]
    holder = jnp.sum(past.astype(jnp.int32), axis=1)
    slot = pair - jnp.sum(jnp.where(past, counts[None, :], 0), axis=1)
    view = holder * requests + slot * 2 + place % 2
    all_images = owners * image_count + locals_
    ids = jnp.arange(all_images.shape[0], dtype=jnp.int32)
    image = jnp.sum(jnp.where(view[:, None] == ids[None, :], all_images[None, :], 0), axis=1)
    owner, row = image // image_count, image % image_count
    gap = (ring_place(owner, worker_count) - ring_place(worker, worker_count)) % worker_count
    middle, half = worker_count // 2, image_count // 2
    late = jnp.logical_and(gap == middle, row >= half)
    part = jnp.where(late, worker_count, gap)
    row = jnp.where(late, row - half, row)
    head = jnp.broadcast_to(jnp.asarray(core, jnp.int32), (8,))
    return jnp.stack([part, row, image, head, jnp.ones_like(image)])


def fetch(table, column, keys, parts, target, sem, wait):
    if wait:
        pltpu.make_async_copy(parts[0].at[0], target, sem).wait()
        return
    part, row = table[0, column], table[1, column]
    for key, source in zip(keys, parts, strict=True):

        @pl.when(part == key)
        def _():
            pltpu.make_async_copy(source.at[row], target, sem).start()


def pick_kernel(keys, first_column, table, *refs):
    parts, (out, sems) = refs[: len(keys)], refs[-2:]
    for wait in (False, True):
        for j in range(4):
            fetch(table, first_column + j, keys, parts, out.at[j], sems.at[j], wait)


def pick(table, parts, first_column, held):
    keys = sorted(parts)
    hold = in_vmem if len(keys) < 10 else in_hbm
    space = pltpu.VMEM if len(keys) < 10 else pltpu.HBM
    _, rows, half = parts[0].shape
    return pl.pallas_call(
        functools.partial(pick_kernel, keys, first_column),
        out_shape=jax.ShapeDtypeStruct((4, rows, half), BF16),
        in_specs=[pl.BlockSpec(memory_space=pltpu.SMEM)]
        + [pl.BlockSpec(memory_space=space)] * len(keys)
        + [pl.BlockSpec(memory_space=pltpu.VMEM)] * len(held),
        out_specs=pl.BlockSpec(memory_space=pl.ANY),
        scratch_shapes=[pltpu.SemaphoreType.DMA((4,))],
        compiler_params=pltpu.CompilerParams(vmem_limit_bytes=8 * 1024 * 1024),
        cost_estimate=pl.CostEstimate(
            flops=0, bytes_accessed=16 * rows * half, transcendentals=0
        ),
        name="pick",
    )(table, *[hold(parts[key]) for key in keys], *[in_vmem(array) for array in held])


def stage_kernel(count, *refs):
    sources, targets, sems = refs[:count], refs[count : 2 * count], refs[2 * count]
    copies = [pltpu.make_async_copy(sources[i], targets[i], sems.at[i]) for i in range(count)]
    for copy in copies:
        copy.start()
    for copy in copies:
        copy.wait()


def stage(arrays):
    count = len(arrays)
    size = sum(array.size * array.dtype.itemsize for array in arrays)
    return pl.pallas_call(
        functools.partial(stage_kernel, count),
        out_shape=tuple(jax.ShapeDtypeStruct(array.shape, array.dtype) for array in arrays),
        in_specs=[pl.BlockSpec(memory_space=pltpu.HBM)] * count,
        out_specs=(pl.BlockSpec(memory_space=pltpu.VMEM),) * count,
        scratch_shapes=[pltpu.SemaphoreType.DMA((count,))],
        compiler_params=pltpu.CompilerParams(vmem_limit_bytes=16 * 1024 * 1024),
        cost_estimate=pl.CostEstimate(flops=0, bytes_accessed=2 * size, transcendentals=0),
        name="stage",
    )(*[in_hbm(array) for array in arrays])


def gather_images(table, parts, held):
    other = lax.ppermute(pick(table, parts, 4, held), "mp", [(0, 1), (1, 0)])
    return pick(table, parts, 0, held), other


def norm_last(rows, gain):
    average = jnp.mean(rows, axis=-1, keepdims=True)
    centered = rows - average
    variance = jnp.mean(centered * centered, axis=-1, keepdims=True)
    return centered * lax.rsqrt(variance + EPS) * gain


def decode_kernel(tokens, table, *refs):
    (mine, theirs, gain_q, gain_c, gain_h, bias_h, wp) = refs[:7]
    wq, wk, wv, wo, wh = refs[7:12]
    outs = refs[12:-8]
    (xq, xc, res, q, k, v, att, hid) = refs[-8:]
    rows, half = mine.shape[1], mine.shape[2]
    views, padded, width = q.shape
    core = table[3, 0]

    for out in outs:
        out[...] = jnp.zeros_like(out)
    tail = jnp.zeros((views, padded - rows, width), BF16)
    att[:, rows:, :] = tail
    res[:, rows:, :] = tail

    here = pl.ds(pl.multiple_of(core * half, half), half)
    there = pl.ds(pl.multiple_of((1 - core) * half, half), half)
    context_of = (1, 0, None, 2) if views == 3 else (1, 0, 3, 2)
    for j in range(4):
        whole, spot = (res, j) if j < views else (att, 0)
        whole[spot, :rows, here] = mine[j]
        whole[spot, :rows, there] = theirs[j]
        full = whole[spot].astype(F32)
        average = jnp.mean(full, axis=-1, keepdims=True)
        full = full - average
        variance = jnp.mean(full * full, axis=-1, keepdims=True)
        full = full * lax.rsqrt(variance + EPS)
        if j < views:
            xq[j] = (full * gain_q[...]).astype(BF16)
        if context_of[j] is not None:
            xc[context_of[j]] = (full * gain_c[...]).astype(BF16)

    total = views * padded
    head_size = width // HEADS
    queries = xq[...].reshape(total, width)
    contexts = xc[...].reshape(total, width)
    proj = jnp.dot(queries, wq[...], preferred_element_type=F32)
    q[...] = (proj.astype(BF16) * BF16(head_size**-0.5)).reshape(views, padded, width)
    proj = jnp.dot(contexts, wk[...], preferred_element_type=F32)
    k[...] = proj.astype(BF16).reshape(views, padded, width)
    proj = jnp.dot(contexts, wv[...], preferred_element_type=F32)
    v[...] = proj.astype(BF16).reshape(views, padded, width)

    block = 2 * head_size
    low = lax.broadcasted_iota(jnp.int32, (padded, block), 1) < head_size
    hide = jnp.where(lax.broadcasted_iota(jnp.int32, (1, padded), 1) < tokens, 0.0, -1e30)
    nothing = jnp.zeros((padded, block), BF16)

    def attend(i, carry):
        for b in range(width // block):
            cols = slice(b * block, (b + 1) * block)
            qb, kb, vb = q[i, :, cols], k[i, :, cols], v[i, :, cols]
            qh = jnp.concatenate([jnp.where(low, qb, nothing), jnp.where(low, nothing, qb)], axis=0)
            scores = lax.dot_general(
                qh, kb, (((1,), (1,)), ((), ())), preferred_element_type=F32
            )
            scores = scores + hide
            peak = jnp.max(scores, axis=-1, keepdims=True)
            expo = jnp.exp(scores - peak)
            inverse = 1.0 / jnp.sum(expo, axis=-1, keepdims=True)
            probs = (expo * inverse).astype(BF16)
            both = jnp.dot(probs, vb, preferred_element_type=F32)
            blended = (both[:padded], both[padded:])
            att[i, :, cols] = jnp.where(low, blended[0], blended[1]).astype(BF16)
        return carry

    if len(outs) == 2:
        for i in range(views):
            attend(i, 0)
    else:
        lax.fori_loop(0, views, attend, 0)

    updated = jnp.dot(att[...].reshape(total, width), wo[...], preferred_element_type=F32)
    updated = updated + res[...].reshape(total, width).astype(F32)
    head_in = norm_last(updated, gain_h[...]).astype(BF16)
    hidden = jnp.dot(head_in, wh[...], preferred_element_type=F32) + bias_h[...]
    hid[...] = jax.nn.gelu(hidden).astype(BF16).reshape(views, padded, hid.shape[2])
    for i in range(views):
        raw = lax.dot_general(
            wp[...], hid[i], (((1,), (1,)), ((), ())), preferred_element_type=F32
        )
        conf = 1.0 + jnp.exp(raw[3:4])
        last = lax.broadcasted_iota(jnp.int32, raw.shape, 0) == 3
        contrib = jnp.where(last, conf, raw * conf)
        contrib = contrib[:, :tokens]
        used = table[4, i] == 1
        if len(outs) == 1:
            image = table[2, i]

            @pl.when(used)
            def _():
                outs[0][image] = outs[0][image] + contrib

            continue
        spot = table[SPOT, i]
        kept = outs[0].shape[0]

        @pl.when(jnp.logical_and(used, spot < kept))
        def _():
            outs[0][spot] = outs[0][spot] + contrib

        @pl.when(jnp.logical_and(used, spot >= kept))
        def _():
            outs[1][spot - kept] = outs[1][spot - kept] + contrib


def per_device(
    tokens,
    gain_query,
    gain_context,
    query_weight,
    key_weight,
    value_weight,
    out_weight,
    gain_head,
    hidden_weight,
    hidden_bias,
    point_weight,
    view_owner,
    view_local,
    pair_count,
):
    worker_count = lax.axis_size("pairs")
    core_count = lax.axis_size("mp")
    worker = lax.axis_index("pairs").astype(jnp.int32)
    core = lax.axis_index("mp").astype(jnp.int32)
    image_count, token_count, half = tokens.shape
    width, hidden_width = hidden_weight.shape
    rows = -(-token_count // 8) * 8
    padded = -(-token_count // 16) * 16

    shard = jnp.pad(tokens, ((0, 0), (0, rows - token_count), (0, 0)))
    scalars = pl.BlockSpec(memory_space=pltpu.SMEM)
    vector = pl.BlockSpec(memory_space=pltpu.VMEM)
    owners = view_owner[:, 0]
    weights = stage((query_weight, key_weight, value_weight, out_weight, hidden_weight))
    vectors = (
        gain_query.reshape(1, width),
        gain_context.reshape(1, width),
        gain_head.reshape(1, width),
        hidden_bias.reshape(1, hidden_width),
        point_weight,
    )

    def decode(views, spots, table, parts, vectors, weights):
        wide = pltpu.VMEM((views, padded, width), BF16)
        keep, other = gather_images(table, parts, weights)
        return pl.pallas_call(
            functools.partial(decode_kernel, token_count),
            out_shape=tuple(
                jax.ShapeDtypeStruct((count, 4, token_count), F32) for count in spots
            ),
            in_specs=[scalars] + [vector] * 12,
            out_specs=(vector,) * len(spots),
            scratch_shapes=[wide] * 7 + [pltpu.VMEM((views, padded, hidden_width), BF16)],
            compiler_params=pltpu.CompilerParams(vmem_limit_bytes=32 * 1024 * 1024),
            name="decode",
        )(table, in_vmem(keep), in_vmem(other), *vectors, *[in_vmem(w) for w in weights])

    swap = [(0, 1), (1, 0)]
    mine = image_count // core_count

    def decode_any(views, table, parts, vectors, weights):
        spots = (worker_count * image_count,)
        (flat,) = decode(views, spots, table, parts, vectors, weights)
        arrived = lax.all_to_all(flat, ("pairs", "mp"), 0, 0, tiled=True)
        arrived = arrived.reshape(worker_count * core_count, mine, 4, token_count)
        return jnp.sum(arrived, axis=0)

    def decode_near(views, table, parts, vectors, weights):
        spots = (3 * image_count, 2 * image_count)
        keep, send = decode(views, spots, table, parts, vectors, weights)
        leaving = keep[: 2 * image_count] + lax.ppermute(send, "mp", swap)
        order = ring_order(worker_count)
        ahead = [
            (order[i] * core_count + c, order[(i + 1 + c) % worker_count] * core_count + c)
            for i in range(worker_count)
            for c in range(core_count)
        ]
        back = [(b, a) for a, b in ahead]
        axes = ("pairs", "mp")
        total = keep[2 * image_count :] + lax.ppermute(leaving[:image_count], axes, ahead)
        total = total + lax.ppermute(leaving[image_count:], axes, back)
        theirs = lax.dynamic_slice_in_dim(total, (1 - core) * mine, mine, 0)
        ours = lax.dynamic_slice_in_dim(total, core * mine, mine, 0)
        return ours + lax.ppermute(theirs, "mp", swap)

    if worker_count == 8:
        reach = 2
        pairs = worker_count * SHARE
        table = pl.pallas_call(
            functools.partial(deal_kernel, worker_count, image_count, reach),
            out_shape=jax.ShapeDtypeStruct((SPOT + 1, 8), jnp.int32),
            in_specs=[scalars] * 4,
            out_specs=scalars,
            scratch_shapes=[pltpu.SMEM((pairs,), jnp.int32)] * 4
            + [pltpu.SMEM((worker_count,), jnp.int32)]
            + [pltpu.SMEM((worker_count * MOST,), jnp.int32)]
            + [pltpu.SMEM((worker_count,), jnp.int32)],
            compiler_params=pltpu.CompilerParams(vmem_limit_bytes=2 * 1024 * 1024),
            cost_estimate=pl.CostEstimate(flops=0, bytes_accessed=20 * 10**6, transcendentals=0),
            name="deal",
        )(owners, view_local, pair_count, jnp.stack([worker, core]))
        parts = ring_near(shard, worker_count, reach)

        def decode_far(table, near, *rest):
            return decode_any(MOST, table, ring_far(near, worker_count, reach), *rest)

        return lax.switch(
            table[LEVEL, 0],
            (
                functools.partial(decode_near, SHARE),
                functools.partial(decode_near, MOST),
                decode_far,
            ),
            table,
            parts,
            vectors,
            weights,
        )
    table = plan(owners, view_local, pair_count, worker, core, image_count, worker_count)
    parts = ring_far({0: shard, worker_count: shard}, worker_count, 0)
    return decode_any(SHARE, table, parts, vectors, weights)


def solution(mesh):
    return jax.shard_map(
        per_device,
        mesh=mesh,
        in_specs=(
            P(("groups", "pairs"), None, "mp"),
            P(),
            P(),
            P(),
            P(),
            P(),
            P(),
            P(),
            P(),
            P(),
            P(),
            P("groups", None),
            P("groups"),
            P("groups"),
        ),
        out_specs=P(("groups", "pairs", "mp"), None, None),
        check_vma=False,
    )
```
